32 devices in a mesh: groups: 2 (over x), space: 16 (over z, y, core).
Axes of the slice: x: 2, y: 2, z: 4, core: 2. Of those that a mesh axis runs over, the one named last changes fastest.
Arguments:
- grid_in: bfloat16 [96, 1440, 128], P(('groups', 'space')), parts along dimension 0, may hold values from -6 to 6
- upstream: bfloat16 [96, 1440, 128], P(('groups', 'space')), parts along dimension 0, may hold values from -6 to 6
- mix_weight: bfloat16 [2, 128, 128], replicated, may hold values from -0.375 to 0.375
- degree_filter: bfloat16 [512, 128], replicated, may hold values from 0.25 to 2
Outputs:
- grad_in: bfloat16 [96, 1440, 128], P(('groups', 'space')), parts along dimension 0
- grad_weight: float32 [4, 128, 128], P('groups'), parts along dimension 0
- grad_filter: float32 [1024, 128], P('groups'), parts along dimension 0
The draws below stay inside these ranges and needn't reach their ends.
There are 2 independent parts, one for each index of `groups`. The reference program is written for one: setup_inputs(seed, part) draws one part's arguments, and reference() takes and returns one part's arrays. A program takes and returns all parts, laid end to end along the dimension named above; an argument that names none is the same for every part. Nothing has to cross between parts.
All inputs are finite; a program needn't handle non-finite values.
Results may differ from the reference program's by a relative error of at most 0.02.
Values may be sent and summed in bfloat16 or wider, within the bound.
A program may use at most 128 MiB of HBM per device.

```python
import math
import jax
import jax.numpy as jnp
from jax import lax

C = 128
NLON = 1440
MODES = 512
NLAT = 48


def block_levels(stream_key, dims, cuts, smallest, high):
    def one(position, parts):
        heights = jax.random.uniform(jax.random.fold_in(jax.random.fold_in(stream_key, 6), position), (parts,), jnp.float32, smallest / len(cuts), high / len(cuts))
        return jnp.repeat(jnp.exp(heights), dims[position] // parts).reshape((-1,) + (1,) * (len(dims) - position - 1))

    gain = one(*cuts[0])
    for cut in cuts[1:]:
        gain = gain * one(*cut)
    return gain


def bell_draw(rng, shape, scale, limit, pieces=(), kind=jnp.bfloat16):
    factor_of = block_levels(rng, shape, pieces, -0.22, 0.18) if pieces else 1.0
    array = jax.random.normal(rng, shape, jnp.float32) * scale * factor_of
    return jnp.minimum(jnp.maximum(array, -limit), limit).astype(kind)


def setup_inputs(seed: int = 0, part: int = 0) -> dict:
    key_list = jax.random.split(jax.random.key(seed), 5)
    part_splits = jax.random.split(jax.random.fold_in(key_list[4], part), 5)
    return {
        "grid_in": bell_draw(part_splits[0], (NLAT, NLON, C), 1.0, 6.0, ((0, 16),)),
        "upstream": bell_draw(part_splits[1], (NLAT, NLON, C), 1.0, 6.0, ((0, 16),)),
        "mix_weight": bell_draw(key_list[2], (2, C, C), (2 * C) ** -0.5, 0.375),
        "degree_filter": jnp.clip(jax.random.uniform(key_list[3], (MODES, C), jnp.float32, 0.25, 2.0), 0.25, 2.0).astype(jnp.bfloat16),
    }


def latitude_angles(lat_count):
    lat_index = jnp.arange(lat_count, dtype=jnp.float32)
    return math.pi * (lat_index + 0.5) / lat_count

def latitude_weights(lat_count):
    return math.pi / lat_count * jnp.sin(latitude_angles(lat_count))

def legendre_rows(m_values, lat_count, mode_count):
    angles = latitude_angles(lat_count)
    cosine = jnp.cos(angles)[None, :]
    sine_lat = jnp.sin(angles)[None, :]
    orders = m_values.astype(jnp.float32)[:, None]
    log_start = 0.5 * (jnp.log(2.0 * orders + 1.0) - math.log(2.0))
    log_start = log_start + 0.5 * (lax.lgamma(2.0 * orders + 1.0) - 2.0 * lax.lgamma(orders + 1.0) - orders * math.log(4.0))
    log_start = log_start + orders * jnp.log(sine_lat)

    def degree_block(carry, block_index):
        p_now, p_prev, log_scale = carry
        outputs = []
        for inner_step in range(32):
            degree = (block_index * 32 + inner_step).astype(jnp.float32)
            active = degree > orders
            denom = jnp.maximum(degree * degree - orders * orders, 1.0)
            coef_a = jnp.sqrt((4.0 * degree * degree - 1.0) / denom)
            lower = jnp.maximum((degree - 1.0) * (degree - 1.0) - orders * orders, 0.0)
            coef_b = jnp.sqrt(lower * (2.0 * degree + 1.0) / (jnp.maximum(2.0 * degree - 3.0, 1.0) * denom))
            p_next = jnp.where(active, coef_a * cosine * p_now - coef_b * p_prev, p_now)
            p_prev = jnp.where(active, p_now, p_prev)
            p_now = p_next
            outputs.append(jnp.where(degree >= orders, p_now * jnp.exp(log_scale), 0.0))
        magnitude = jnp.maximum(jnp.abs(p_now), jnp.abs(p_prev))
        next_carry = (p_now / magnitude, p_prev / magnitude, log_scale + jnp.log(magnitude))
        return (next_carry, jnp.stack(outputs, 1))
    ones_grid = jnp.ones((m_values.shape[0], lat_count), jnp.float32)
    start_carry = (ones_grid, jnp.zeros_like(ones_grid), log_start * ones_grid)
    block_ids = jnp.arange(mode_count // 32, dtype=jnp.int32)
    final_carry, stacked = lax.scan(degree_block, start_carry, block_ids)
    return jnp.transpose(stacked, (1, 0, 2, 3)).reshape(m_values.shape[0], mode_count, lat_count)

def fourier_tables(m_order, lon_count):
    lon_index = jnp.arange(lon_count, dtype=jnp.int32)
    phases = m_order[:, None] * lon_index[None, :] % lon_count
    angles = 2.0 * math.pi / lon_count * phases.astype(jnp.float32)
    factor = 1.0 / math.sqrt(lon_count)
    analysis = jnp.stack([jnp.cos(angles) * factor, -jnp.sin(angles) * factor], 1)
    analysis = analysis.reshape(2 * m_order.shape[0], lon_count).astype(jnp.bfloat16)
    doubling = jnp.where(m_order == 0, 1.0, 2.0).astype(jnp.bfloat16)
    synthesis = analysis * jnp.repeat(doubling, 2)[:, None]
    return (analysis, synthesis)

def mixing_matrix(mix_weight):
    upper = jnp.concatenate([mix_weight[0], mix_weight[1]], 1)
    lower = jnp.concatenate([-mix_weight[1], mix_weight[0]], 1)
    return jnp.concatenate([upper, lower], 0)

def fold_weight(block_grad):
    half = block_grad.shape[0] // 2
    real_part = block_grad[:half, :half] + block_grad[half:, half:]
    imag_part = block_grad[:half, half:] - block_grad[half:, :half]
    return jnp.stack([real_part, imag_part], 0)

def gelu_slope(field):
    return 0.5 * (1.0 + lax.erf(field * (1.0 / math.sqrt(2.0)))) + field * jnp.exp(-0.5 * field * field) * (1.0 / math.sqrt(2.0 * math.pi))

def product(form, left, right):
    return jnp.einsum(form, left.astype(jnp.float32), right.astype(jnp.float32), precision=lax.Precision.HIGHEST)

def reference(grid_in, upstream, mix_weight, degree_filter):
    lat_count, lon_count, channels = grid_in.shape
    positions = jnp.arange(MODES, dtype=jnp.int32)
    analysis, synthesis = fourier_tables(positions, lon_count)
    wide_weight = mixing_matrix(mix_weight)
    filter_gain = degree_filter.astype(jnp.float32)
    lat_weight = latitude_weights(lat_count)
    block_count = MODES // 32
    block_ids = jnp.arange(block_count, dtype=jnp.int32)
    fourier = product('kn,anc->akc', analysis, grid_in).astype(jnp.bfloat16)
    fourier_blocks = jnp.transpose(fourier.reshape(lat_count, block_count, 32, 2 * channels), (1, 0, 2, 3))

    def forward_pass(block_index, fourier_part):
        m_values = block_index * 32 + jnp.arange(32, dtype=jnp.int32)
        legendre = legendre_rows(m_values, lat_count, MODES)
        synth_table = legendre.astype(jnp.bfloat16)
        anal_table = (legendre * lat_weight).astype(jnp.bfloat16)
        spectrum = product('jla,ajx->jlx', anal_table, fourier_part).astype(jnp.bfloat16)
        scaled = (spectrum.reshape(32, MODES, 2, channels).astype(jnp.float32) * filter_gain[None, :, None, :]).astype(jnp.bfloat16)
        scaled_rows = scaled.reshape(32 * MODES, 2 * channels)
        mixed = jnp.dot(scaled_rows, wide_weight, preferred_element_type=jnp.float32).astype(jnp.bfloat16)
        return (synth_table, anal_table, spectrum, scaled_rows, mixed)

    def forward_block(operands):
        block_index, fourier_part = operands
        synth_table, anal_table, spectrum, scaled_rows, mixed = forward_pass(block_index, fourier_part)
        return product('jla,jlx->ajx', synth_table, mixed.reshape(32, MODES, 2 * channels)).astype(jnp.bfloat16)
    returned = lax.map(forward_block, (block_ids, fourier_blocks))
    returned = jnp.transpose(returned, (1, 0, 2, 3)).reshape(lat_count, 2 * MODES, channels)
    field = product('kn,akc->anc', synthesis, returned)
    slope = (upstream.astype(jnp.float32) * gelu_slope(field)).astype(jnp.bfloat16)
    gfourier = product('kn,anc->akc', synthesis, slope).astype(jnp.bfloat16)
    gradient_blocks = jnp.transpose(gfourier.reshape(lat_count, block_count, 32, 2 * channels), (1, 0, 2, 3))

    def backward_block(operands):
        block_index, fourier_part, gradient_part = operands
        synth_table, anal_table, spectrum, scaled_rows, mixed = forward_pass(block_index, fourier_part)
        gmixed = product('jla,ajx->jlx', synth_table, gradient_part).astype(jnp.bfloat16)
        gmixed_rows = gmixed.reshape(32 * MODES, 2 * channels)
        weight_part = lax.dot_general(scaled_rows, gmixed_rows, (((0,), (0,)), ((), ())), preferred_element_type=jnp.float32)
        gscaled = lax.dot_general(gmixed_rows, wide_weight, (((1,), (1,)), ((), ())), preferred_element_type=jnp.float32)
        gscaled = gscaled.reshape(32, MODES, 2, channels)
        filter_part = lax.optimization_barrier(jnp.sum(gscaled * spectrum.reshape(32, MODES, 2, channels).astype(jnp.float32), axis=(0, 2)))
        gspectrum = (gscaled * filter_gain[None, :, None, :]).astype(jnp.bfloat16).reshape(32, MODES, 2 * channels)
        gfield = product('jla,jlx->ajx', anal_table, gspectrum).astype(jnp.bfloat16)
        return (gfield, weight_part, filter_part)
    gfields, weight_parts, filter_parts = lax.map(backward_block, (block_ids, fourier_blocks, gradient_blocks))
    gfields = jnp.transpose(gfields, (1, 0, 2, 3)).reshape(lat_count, 2 * MODES, channels)
    grad_in = (product('kn,akc->anc', analysis, gfields) + upstream.astype(jnp.float32)).astype(jnp.bfloat16)
    grad_weight = fold_weight(lax.optimization_barrier(jnp.sum(weight_parts, 0))) * (1.0 / MODES)
    grad_filter = lax.optimization_barrier(jnp.sum(filter_parts, 0)) * 0.125
    return (grad_in, grad_weight, grad_filter)
```

```python
import functools
import math

import jax
import jax.numpy as jnp
from jax import lax
from jax.experimental import pallas as pl
from jax.experimental.pallas import tpu as pltpu
from jax.sharding import PartitionSpec as P

MODES = 512
ROWS = 32
F32 = jnp.float32
BF16 = jnp.bfloat16


def params(**extra):
    return pltpu.CompilerParams(vmem_limit_bytes=56 * 1024 * 1024, **extra)


def latitude_angles(index, lat_count):
    return math.pi * (index.astype(F32) + 0.5) / lat_count


def row_phase(rows, devices, lon_count):
    slots = MODES // devices
    device = rows // (2 * slots)
    part = rows // slots % 2
    order = rows % slots * devices + device
    return order, part * (lon_count // 4)


def trig(phases, lon_count):
    angles = 2.0 * math.pi / lon_count * (phases % lon_count).astype(F32)
    return jnp.stack([jnp.cos(angles), jnp.sin(angles)], 0)


def base_tables(devices, lon_count):
    total = 2 * MODES
    lon = jnp.arange(lon_count, dtype=jnp.int32)
    factor = 1.0 / math.sqrt(lon_count)
    order, offset = row_phase(jnp.arange(total, dtype=jnp.int32), devices, lon_count)
    fine = order[:ROWS, None] * lon[None, :] + offset[:ROWS, None]
    coarse = order[::ROWS, None] * lon[None, :] + offset[::ROWS, None]
    tfine = lon[:ROWS, None] * order[None, :] + offset[None, :]
    tcoarse = lon[::ROWS, None] * order[None, :]
    return (
        trig(coarse, lon_count),
        trig(fine, lon_count) * factor,
        trig(tcoarse, lon_count),
        trig(tfine, lon_count) * factor,
    )


def fourier_kernel(coarse, fine, tcoarse, tfine, grid, table, ttable, out):
    lat_local = grid.shape[0]
    devices, span = out.shape[0], out.shape[1]

    def fill(dst, big, small):
        def step(h, carry):
            value = big[0, pl.ds(h, 1), :] * small[0] - big[1, pl.ds(h, 1), :] * small[1]
            dst[pl.ds(pl.multiple_of(h * ROWS, ROWS), ROWS), :] = value.astype(BF16)
            return carry

        lax.fori_loop(0, big.shape[1], step, 0)

    fill(table, coarse, fine)
    fill(ttable, tcoarse, tfine)
    wide = jnp.concatenate([grid[a] for a in range(lat_local)], 1)
    chunk = 256

    def product(q, carry):
        rows = pl.ds(pl.multiple_of(q * chunk, chunk), chunk)
        value = jnp.dot(table[rows, :], wide, preferred_element_type=F32)
        value = value.astype(BF16).reshape(chunk // span, span, value.shape[1])
        out[pl.ds(q * (chunk // span), chunk // span)] = value
        return carry

    lax.fori_loop(0, 2 * MODES // chunk, product, 0)


def legendre_kernel(order_ref, cos_ref, start_ref, weight_ref, wcol_ref, synth, anal, tsynth, tanal, hold):
    groups, width = order_ref.shape
    orders = order_ref[...]
    order_sq = orders * orders
    cosine = cos_ref[...]
    weight = weight_ref[...]
    block = 32

    def degree_block(index, carry):
        p_now, p_prev, e_prev, log_scale = carry
        scale = jnp.exp(log_scale)
        base = index * block
        for inner in range(block):
            degree_int = base + inner
            degree = degree_int.astype(F32)
            active = degree > orders
            square = degree * degree
            ratio = jnp.maximum(square - order_sq, 1.0) / jnp.maximum(4.0 * square - 1.0, 1.0)
            coef = lax.rsqrt(ratio)
            p_next = jnp.where(active, coef * (cosine * p_now - e_prev * p_prev), p_now)
            p_prev = jnp.where(active, p_now, p_prev)
            e_prev = jnp.where(active, ratio * coef, 0.0)
            p_now = p_next
            value = jnp.where(degree >= orders, p_now * scale, 0.0)
            rows = pl.ds(pl.multiple_of(degree_int * groups, groups), groups)
            for part in range(width // 128):
                hold[part, rows, :] = value[:, part * 128 : (part + 1) * 128]
        magnitude = jnp.maximum(jnp.abs(p_now), jnp.abs(p_prev))
        return (p_now / magnitude, p_prev / magnitude, e_prev, log_scale + jnp.log(magnitude))

    ones = jnp.ones((groups, width), F32)
    zeros = jnp.zeros((groups, width), F32)
    lax.fori_loop(0, MODES // block, degree_block, (ones, zeros, zeros, start_ref[...]))

    def spread(g, carry):
        wrow = weight[0:1, :]
        pieces = [
            hold[part, pl.ds(g, MODES, stride=groups), :]
            for part in range(width // 128)
        ]
        value = pieces[0] if len(pieces) == 1 else jnp.concatenate(pieces, 1)
        synth[g] = value.astype(BF16)
        anal[g] = (value * wrow).astype(BF16)
        turned = value.T
        tsynth[g] = turned.astype(BF16)
        tanal[g] = (turned * wcol_ref[:, 0:1]).astype(BF16)
        return carry

    lax.fori_loop(0, synth.shape[0], spread, 0)


def unpack(src, scratch):
    devices, span, _ = src.shape
    for a in range(scratch.shape[0]):
        part = src[:, :, a * 128 : (a + 1) * 128].astype(F32)
        scratch[a] = part.reshape(devices * span, 128)


def pack(scratch, dst):
    devices, span, _ = dst.shape
    for a in range(scratch.shape[0]):
        dst[:, :, a * 128 : (a + 1) * 128] = (
            scratch[a].reshape(devices, span, 128).astype(BF16)
        )


def gather_group(scratch, g, devices, span, per_group, height):
    lat_local = scratch.shape[0]
    slots = span // 2
    rows = []
    for j in range(per_group):
        s = g * per_group + j
        halves = []
        for r in range(2):
            parts = [
                scratch[a, pl.ds(r * slots + s, devices, stride=span), :] for a in range(lat_local)
            ]
            if height > devices * lat_local:
                parts.append(jnp.zeros((height - devices * lat_local, 128), F32))
            halves.append(jnp.concatenate(parts, 0))
        zero = jnp.zeros((height, 256), F32)
        cells = [zero] * per_group
        cells[j] = jnp.concatenate(halves, 1)
        rows.append(cells[0] if per_group == 1 else jnp.concatenate(cells, 1))
    return (rows[0] if per_group == 1 else jnp.concatenate(rows, 0)).astype(BF16)


def scatter_group(value, scratch, g, devices, span, per_group, height):
    lat_local = scratch.shape[0]
    slots = span // 2
    for j in range(per_group):
        s = g * per_group + j
        for r in range(2):
            for a in range(lat_local):
                top = j * height + a * devices
                left = j * 256 + r * 128
                scratch[a, pl.ds(r * slots + s, devices, stride=span), :] = value[
                    top : top + devices, left : left + 128
                ]


def over_groups(groups, body):
    sections = 4
    each = groups // sections
    for q in range(sections):
        first = q * (MODES // sections)
        lax.fori_loop(q * each, (q + 1) * each, functools.partial(body, first), 0)


def widen(filter_ref, first, copies):
    gain = filter_ref[first:, :].astype(F32)
    return jnp.concatenate([gain] * copies, 1)


def forward_kernel(per_group, src, anal, tsynth, filt, weight, out, scratch, back):
    devices, span, _ = src.shape
    groups, _, width = anal.shape
    height = width // per_group
    unpack(src, scratch)

    def body(first, g, carry):
        operand = gather_group(scratch, g, devices, span, per_group, height)
        spectrum = jnp.dot(anal[g, first:, :], operand, preferred_element_type=F32).astype(BF16)
        scaled = (spectrum.astype(F32) * widen(filt, first, 2 * per_group)).astype(BF16)
        mixed = [
            jnp.dot(
                scaled[:, j * 256 : (j + 1) * 256], weight[...], preferred_element_type=F32
            ).astype(BF16)
            for j in range(per_group)
        ]
        mixed = mixed[0] if per_group == 1 else jnp.concatenate(mixed, 1)
        value = jnp.dot(tsynth[g, :, first:], mixed, preferred_element_type=F32)
        scatter_group(value, back, g, devices, span, per_group, height)
        return carry

    over_groups(groups, body)
    pack(back, out)


def backward_kernel(
    per_group, src, gsrc, anal, synth, tanal, filt, weight, out, wgrad, fgrad, scratch, gscratch
):
    devices, span, _ = src.shape
    groups, _, width = anal.shape
    height = width // per_group
    unpack(src, scratch)
    unpack(gsrc, gscratch)
    wgrad[...] = jnp.zeros_like(wgrad)
    fgrad[...] = jnp.zeros_like(fgrad)

    def body(first, g, carry):
        operand = gather_group(scratch, g, devices, span, per_group, height)
        goperand = gather_group(gscratch, g, devices, span, per_group, height)
        gain = widen(filt, first, 2)
        outs = []
        spectrum = jnp.dot(anal[g, first:, :], operand, preferred_element_type=F32).astype(BF16)
        gmixed = jnp.dot(synth[g, first:, :], goperand, preferred_element_type=F32).astype(BF16)
        for j in range(per_group):
            lanes = slice(j * 256, (j + 1) * 256)
            spec = spectrum[:, lanes].astype(F32)
            scaled = (spec * gain).astype(BF16)
            gmix = gmixed[:, lanes]
            wgrad[...] += lax.dot_general(
                scaled, gmix, (((0,), (0,)), ((), ())), preferred_element_type=F32
            )
            gscaled = lax.dot_general(
                gmix, weight[...], (((1,), (1,)), ((), ())), preferred_element_type=F32
            )
            term = gscaled * spec
            fgrad[first:, :] += term[:, :128] + term[:, 128:]
            outs.append((gscaled * gain).astype(BF16))
        gspectrum = outs[0] if per_group == 1 else jnp.concatenate(outs, 1)
        value = jnp.dot(tanal[g, :, first:], gspectrum, preferred_element_type=F32)
        scatter_group(value, scratch, g, devices, span, per_group, height)
        return carry

    over_groups(groups, body)
    pack(scratch, out)


def gelu_slope(field):
    return 0.5 * (1.0 + lax.erf(field * (1.0 / math.sqrt(2.0)))) + field * jnp.exp(
        -0.5 * field * field
    ) * (1.0 / math.sqrt(2.0 * math.pi))


LON_CHUNK = 288


def merged(src):
    devices, span, width = src.shape
    return src[...].astype(F32).reshape(devices * span, width)


def slope_kernel(src, alpha, table, ttable, upstream, out, slope):
    lat_local, lon_count, channels = upstream.shape
    devices, span, _ = out.shape
    operand = (merged(src) * alpha[:, 0:1]).astype(BF16)

    def grid_rows(q, carry):
        rows = pl.ds(pl.multiple_of(q * LON_CHUNK, LON_CHUNK), LON_CHUNK)
        field = jnp.dot(ttable[rows, :], operand, preferred_element_type=F32)
        up = jnp.concatenate([upstream[a, rows, :] for a in range(lat_local)], 1)
        slope[rows, :] = (up.astype(F32) * gelu_slope(field)).astype(BF16)
        return carry

    lax.fori_loop(0, lon_count // LON_CHUNK, grid_rows, 0)
    chunk = 256

    def product(q, carry):
        rows = pl.ds(pl.multiple_of(q * chunk, chunk), chunk)
        value = jnp.dot(table[rows, :], slope[...], preferred_element_type=F32)
        value = (value * alpha[rows, 0:1]).astype(BF16)
        out[pl.ds(q * (chunk // span), chunk // span)] = value.reshape(
            chunk // span, span, value.shape[1]
        )
        return carry

    lax.fori_loop(0, 2 * MODES // chunk, product, 0)


def final_kernel(src, ttable, upstream, out):
    lat_local, lon_count, channels = upstream.shape
    operand = merged(src).astype(BF16)

    def grid_rows(q, carry):
        rows = pl.ds(pl.multiple_of(q * LON_CHUNK, LON_CHUNK), LON_CHUNK)
        value = jnp.dot(ttable[rows, :], operand, preferred_element_type=F32)
        for a in range(lat_local):
            part = value[:, a * channels : (a + 1) * channels]
            out[a, rows, :] = (part + upstream[a, rows, :].astype(F32)).astype(BF16)
        return carry

    lax.fori_loop(0, lon_count // LON_CHUNK, grid_rows, 0)


def mixing_matrix(mix_weight):
    upper = jnp.concatenate([mix_weight[0], mix_weight[1]], 1)
    lower = jnp.concatenate([-mix_weight[1], mix_weight[0]], 1)
    return jnp.concatenate([upper, lower], 0)


def fold_weight(block_grad):
    half = block_grad.shape[0] // 2
    real_part = block_grad[:half, :half] + block_grad[half:, half:]
    imag_part = block_grad[:half, half:] - block_grad[half:, :half]
    return jnp.concatenate([real_part, imag_part], 0)


def exchange(value):
    return lax.all_to_all(value, "space", split_axis=0, concat_axis=0, tiled=True)


def shape(dims, kind=BF16):
    return jax.ShapeDtypeStruct(dims, kind)


def body(grid_in, upstream, mix_weight, degree_filter):
    devices = lax.axis_size("space")
    me = lax.axis_index("space")
    lat_local, lon_count, channels = grid_in.shape
    lat_count = lat_local * devices
    slots = MODES // devices
    span = 2 * slots
    height = 64 if lat_count <= 64 else -(-lat_count // 128) * 128
    per_group = 128 // height if height < 128 else 1
    width = height * per_group
    groups = slots // per_group
    packet = shape((devices, span, lat_local * channels))

    table, ttable, fourier = pl.pallas_call(
        fourier_kernel,
        out_shape=(shape((2 * MODES, lon_count)), shape((lon_count, 2 * MODES)), packet),
        compiler_params=params(),
        name="fourier_stage",
    )(*base_tables(devices, lon_count), grid_in)
    spectral_in = exchange(fourier)

    lane = jnp.arange(width, dtype=jnp.int32)
    within = lane % height
    valid = within < lat_count
    latitude = jnp.where(valid, within % devices * lat_local + within // devices, 0)
    angles = latitude_angles(latitude, lat_count)
    group = jnp.minimum(jnp.arange(-(-groups // 8) * 8, dtype=jnp.int32), groups - 1)[:, None]
    orders = ((group * per_group + lane[None, :] // height) * devices + me).astype(F32)
    cosine = jnp.broadcast_to(jnp.cos(angles)[None, :], orders.shape)
    start = 0.5 * (jnp.log(2.0 * orders + 1.0) - math.log(2.0))
    start = start + 0.5 * (
        lax.lgamma(2.0 * orders + 1.0) - 2.0 * lax.lgamma(orders + 1.0) - orders * math.log(4.0)
    )
    start = start + orders * jnp.log(jnp.sin(angles))[None, :]
    weights = jnp.where(valid, math.pi / lat_count * jnp.sin(angles), 0.0)
    tall = shape((groups, MODES, width))
    flat = shape((groups, width, MODES))
    synth, anal, tsynth, tanal = pl.pallas_call(
        legendre_kernel,
        out_shape=(tall, tall, flat, flat),
        scratch_shapes=[pltpu.VMEM((width // 128, MODES * orders.shape[0], 128), F32)],
        compiler_params=params(),
        name="legendre_stage",
    )(
        orders,
        cosine,
        start,
        jnp.broadcast_to(weights[None, :], (8, width)),
        jnp.broadcast_to(weights[:, None], (width, 128)),
    )

    wide_weight = mixing_matrix(mix_weight)
    slab = pltpu.VMEM((lat_local, devices * span, 128), F32)
    grid_modes = pl.pallas_call(
        functools.partial(forward_kernel, per_group),
        out_shape=packet,
        scratch_shapes=[slab, slab],
        compiler_params=params(),
        name="forward_stage",
    )(spectral_in, anal, tsynth, degree_filter, wide_weight)
    returned = exchange(grid_modes)

    order, _ = row_phase(jnp.arange(2 * MODES, dtype=jnp.int32), devices, lon_count)
    alpha = jnp.broadcast_to(jnp.where(order == 0, 1.0, 2.0).astype(F32)[:, None], (2 * MODES, 128))
    gfourier = pl.pallas_call(
        slope_kernel,
        out_shape=packet,
        scratch_shapes=[pltpu.VMEM((lon_count, lat_local * channels), BF16)],
        compiler_params=params(),
        name="slope_stage",
    )(returned, alpha, table, ttable, upstream)
    gradient_in = exchange(gfourier)

    gfield_modes, weight_total, filter_total = pl.pallas_call(
        functools.partial(backward_kernel, per_group),
        out_shape=(packet, shape((2 * channels, 2 * channels), F32), shape((MODES, channels), F32)),
        scratch_shapes=[slab, slab],
        compiler_params=params(),
        name="backward_stage",
    )(spectral_in, gradient_in, anal, synth, tanal, degree_filter, wide_weight)
    gfield = exchange(gfield_modes)
    totals = jnp.concatenate(
        [fold_weight(weight_total) * (1.0 / MODES), filter_total * 0.125], 0
    ).reshape(devices, -1, channels)
    share = jnp.sum(exchange(totals), 0)
    summed = exchange(jnp.broadcast_to(share[None], (devices,) + share.shape))
    summed = summed.reshape(2 * channels + MODES, channels)

    grad_in = pl.pallas_call(
        final_kernel,
        out_shape=shape(grid_in.shape),
        compiler_params=params(),
        name="final_stage",
    )(gfield, ttable, upstream)
    return (
        grad_in,
        summed[: 2 * channels].reshape(2, channels, channels),
        summed[2 * channels :],
    )


def solution(mesh):
    return jax.shard_map(
        body,
        mesh=mesh,
        in_specs=(P(("groups", "space"), None, None), P(("groups", "space"), None, None), P(), P()),
        out_specs=(P(("groups", "space"), None, None), P("groups", None, None), P("groups", None)),
        check_vma=False,
    )
```

```python
import functools
import math

import jax
import jax.numpy as jnp
from jax import lax
from jax.experimental import pallas as pl
from jax.experimental.pallas import tpu as pltpu
from jax.sharding import PartitionSpec as P

MODES = 512
ROWS = 32
F32 = jnp.float32
BF16 = jnp.bfloat16


def params(**extra):
    return pltpu.CompilerParams(vmem_limit_bytes=56 * 1024 * 1024, **extra)


def latitude_angles(index, lat_count):
    return math.pi * (index.astype(F32) + 0.5) / lat_count


def greet(devices):
    me = lax.axis_index("space")
    barrier = pltpu.get_barrier_semaphore()

    def hello(step, carry):
        peer = (me + step) % devices
        pl.semaphore_signal(
            barrier, inc=1, device_id={"space": peer}, device_id_type=pl.DeviceIdType.MESH
        )
        return carry

    lax.fori_loop(1, devices, hello, 0)


def await_greetings(devices):
    pl.semaphore_wait(pltpu.get_barrier_semaphore(), devices - 1)


def remote(src, dst, send_sem, recv_sem, peer):
    return pltpu.make_async_remote_copy(
        src_ref=src,
        dst_ref=dst,
        send_sem=send_sem,
        recv_sem=recv_sem,
        device_id={"space": peer},
        device_id_type=pl.DeviceIdType.MESH,
    )


class Exchange:
    def __init__(self, source, target, send_sem, recv_sem):
        self.source, self.target = source, target
        self.send_sem, self.recv_sem = send_sem, recv_sem
        self.devices = source.shape[1]
        self.me = lax.axis_index("space")

    def copy(self, section, step):
        peer = (self.me + step) % self.devices
        return remote(
            self.source.at[section, peer],
            self.target.at[section, self.me],
            self.send_sem.at[section, step],
            self.recv_sem.at[section, step],
            peer,
        )

    def send(self, section):
        half = self.devices // 2

        def one(index, carry):
            sign = 1 - 2 * (index % 2)
            step = (half + sign * ((index + 1) // 2) + self.devices) % self.devices
            self.copy(section, step).start()
            return carry

        lax.fori_loop(0, self.devices - 1, one, 0)
        self.target[section, self.me] = self.source[section, self.me]

    def finish(self):
        for section in range(self.source.shape[0]):

            def one(step, carry, section=section):
                copy = self.copy(section, step)
                copy.wait_recv()
                copy.wait_send()
                return carry

            lax.fori_loop(1, self.devices, one, 0)


def reduce_all(red, inbox, total, send_sem, recv_sem):
    devices = red.shape[0]
    me = lax.axis_index("space")
    base = me * 0
    steps = []
    stride = 1
    while stride < devices:
        half = devices // (2 * stride)
        bit = me // stride % 2
        partner = me + (1 - 2 * bit) * stride
        steps.append((half, bit, partner))
        stride *= 2
    trail = []
    for t, (half, bit, partner) in enumerate(steps):
        keep = base + bit * half
        give = base + (1 - bit) * half
        copy = remote(
            red.at[pl.ds(give, half)],
            inbox.at[pl.ds(half, half)],
            send_sem.at[t],
            recv_sem.at[t],
            partner,
        )
        copy.start()
        copy.wait()
        red[pl.ds(keep, half)] += inbox[half : 2 * half]
        base = keep
        trail.append(base)
    total[pl.ds(base, 1)] = red[pl.ds(base, 1)]
    count = len(steps)
    for t in reversed(range(count)):
        half, bit, partner = steps[t]
        block = pl.ds(trail[t], half)
        copy = remote(
            total.at[block],
            total.at[block],
            send_sem.at[count + t],
            recv_sem.at[count + t],
            partner,
        )
        copy.start()
        copy.wait()


def sections_of(devices):
    return max(1, min(4, MODES // devices // 8))


def row_phase(rows, devices, lon_count):
    span = 2 * MODES // devices // sections_of(devices)
    section = rows // (span * devices)
    device = rows // span % devices
    part = rows // (span // 2) % 2
    slot = section * (span // 2) + rows % (span // 2)
    return slot * devices + device, part * (lon_count // 4)


def trig(phases, lon_count):
    angles = 2.0 * math.pi / lon_count * (phases % lon_count).astype(F32)
    return jnp.stack([jnp.cos(angles), jnp.sin(angles)], 0)


def base_tables(devices, lon_count):
    total = 2 * MODES
    lon = jnp.arange(lon_count, dtype=jnp.int32)
    factor = 1.0 / math.sqrt(lon_count)
    order, offset = row_phase(jnp.arange(total, dtype=jnp.int32), devices, lon_count)
    fine = order[:ROWS, None] * lon[None, :] + offset[:ROWS, None]
    coarse = order[::ROWS, None] * lon[None, :] + offset[::ROWS, None]
    tfine = lon[:ROWS, None] * order[None, :] + offset[None, :]
    tcoarse = lon[::ROWS, None] * order[None, :]
    return (
        trig(coarse, lon_count),
        trig(fine, lon_count) * factor,
        trig(tcoarse, lon_count),
        trig(tfine, lon_count) * factor,
    )


def fill(dst, big, small):
    def step(h, carry):
        value = big[0, pl.ds(h, 1), :] * small[0] - big[1, pl.ds(h, 1), :] * small[1]
        dst[pl.ds(pl.multiple_of(h * ROWS, ROWS), ROWS), :] = value.astype(BF16)
        return carry

    lax.fori_loop(0, big.shape[1], step, 0)


def section_product(table, wide, out, section, scale=None):
    _, devices, span, width = out.shape
    chunk = 256
    each = chunk // span

    def product(q, carry):
        rows = pl.ds(pl.multiple_of(section * devices * span + q * chunk, chunk), chunk)
        value = jnp.dot(table[rows, :], wide, preferred_element_type=F32)
        if scale is not None:
            value = value * scale[rows, 0:1]
        out[section, pl.ds(q * each, each)] = value.astype(BF16).reshape(each, span, width)
        return carry

    lax.fori_loop(0, devices * span // chunk, product, 0)


def fourier_kernel(
    coarse, fine, tcoarse, tfine, grid, order_ref, cos_ref, start_ref, weight_ref, wcol_ref,
    table, ttable, received, synth, anal, tsynth, tanal,
    out, hold, send_sem, recv_sem,
):
    sections, devices = out.shape[:2]
    greet(devices)
    fill(table, coarse, fine)
    wide = jnp.concatenate([grid[a] for a in range(grid.shape[0])], 1)
    exchange = Exchange(out, received, send_sem, recv_sem)
    for section in range(sections):
        section_product(table, wide, out, section)
        if section == 0:
            await_greetings(devices)
        exchange.send(section)
    legendre_tables(
        order_ref, cos_ref, start_ref, weight_ref, wcol_ref, synth, anal, tsynth, tanal, hold
    )
    fill(ttable, tcoarse, tfine)
    exchange.finish()


def legendre_tables(
    order_ref, cos_ref, start_ref, weight_ref, wcol_ref, synth, anal, tsynth, tanal, hold
):
    groups, width = order_ref.shape
    orders = order_ref[...]
    order_sq = orders * orders
    cosine = cos_ref[...]
    weight = weight_ref[...]
    block = 32

    def degree_block(index, carry):
        p_now, p_prev, e_prev, log_scale = carry
        scale = jnp.exp(log_scale)
        base = index * block
        for inner in range(block):
            degree_int = base + inner
            degree = degree_int.astype(F32)
            active = degree > orders
            square = degree * degree
            ratio = jnp.maximum(square - order_sq, 1.0) / jnp.maximum(4.0 * square - 1.0, 1.0)
            coef = lax.rsqrt(ratio)
            p_next = jnp.where(active, coef * (cosine * p_now - e_prev * p_prev), p_now)
            p_prev = jnp.where(active, p_now, p_prev)
            e_prev = jnp.where(active, ratio * coef, 0.0)
            p_now = p_next
            value = jnp.where(degree >= orders, p_now * scale, 0.0)
            rows = pl.ds(pl.multiple_of(degree_int * groups, groups), groups)
            for part in range(width // 128):
                hold[part, rows, :] = value[:, part * 128 : (part + 1) * 128]
        magnitude = jnp.maximum(jnp.abs(p_now), jnp.abs(p_prev))
        return (p_now / magnitude, p_prev / magnitude, e_prev, log_scale + jnp.log(magnitude))

    ones = jnp.ones((groups, width), F32)
    zeros = jnp.zeros((groups, width), F32)
    lax.fori_loop(0, MODES // block, degree_block, (ones, zeros, zeros, start_ref[...]))

    def spread(g, carry):
        wrow = weight[0:1, :]
        pieces = [
            hold[part, pl.ds(g, MODES, stride=groups), :]
            for part in range(width // 128)
        ]
        value = pieces[0] if len(pieces) == 1 else jnp.concatenate(pieces, 1)
        synth[g] = value.astype(BF16)
        anal[g] = (value * wrow).astype(BF16)
        turned = value.T
        tsynth[g] = turned.astype(BF16)
        tanal[g] = (turned * wcol_ref[:, 0:1]).astype(BF16)
        return carry

    lax.fori_loop(0, synth.shape[0], spread, 0)


def unpack(src, scratch):
    sections, devices, span, _ = src.shape
    for q in range(sections):
        for a in range(scratch.shape[0]):
            part = src[q, :, :, a * 128 : (a + 1) * 128].astype(F32)
            scratch[a, q * devices * span : (q + 1) * devices * span] = part.reshape(
                devices * span, 128
            )


def pack(scratch, dst, q):
    _, devices, span, _ = dst.shape
    for a in range(scratch.shape[0]):
        part = scratch[a, q * devices * span : (q + 1) * devices * span]
        dst[q, :, :, a * 128 : (a + 1) * 128] = part.reshape(devices, span, 128).astype(BF16)


def strided_rows(s, r, devices, span):
    half = span // 2
    start = s // half * (devices * span) + r * half + s % half
    return pl.ds(start, devices, stride=span)


def gather_group(scratch, g, devices, span, per_group, height):
    lat_local = scratch.shape[0]
    rows = []
    for j in range(per_group):
        s = g * per_group + j
        halves = []
        for r in range(2):
            pick = strided_rows(s, r, devices, span)
            parts = [scratch[a, pick, :] for a in range(lat_local)]
            if height > devices * lat_local:
                parts.append(jnp.zeros((height - devices * lat_local, 128), F32))
            halves.append(jnp.concatenate(parts, 0))
        zero = jnp.zeros((height, 256), F32)
        cells = [zero] * per_group
        cells[j] = jnp.concatenate(halves, 1)
        rows.append(cells[0] if per_group == 1 else jnp.concatenate(cells, 1))
    return (rows[0] if per_group == 1 else jnp.concatenate(rows, 0)).astype(BF16)


def scatter_group(value, scratch, g, devices, span, per_group, height):
    lat_local = scratch.shape[0]
    for j in range(per_group):
        s = g * per_group + j
        for r in range(2):
            for a in range(lat_local):
                top = j * height + a * devices
                left = j * 256 + r * 128
                scratch[a, strided_rows(s, r, devices, span), :] = value[
                    top : top + devices, left : left + 128
                ]


def over_groups(groups, sections, body, after):
    pieces = 4
    each = groups // pieces
    for q in range(pieces):
        first = q * (MODES // pieces)
        lax.fori_loop(q * each, (q + 1) * each, functools.partial(body, first), 0)
        if (q + 1) % (pieces // sections) == 0:
            after(q // (pieces // sections))


def widen(filter_ref, first, copies):
    gain = filter_ref[first:, :].astype(F32)
    return jnp.concatenate([gain] * copies, 1)


def forward_kernel(
    per_group, src, anal, tsynth, filt, weight, received, out, scratch, back, send_sem, recv_sem
):
    sections, devices, span, _ = src.shape
    groups, _, width = anal.shape
    height = width // per_group
    greet(devices)
    unpack(src, scratch)
    exchange = Exchange(out, received, send_sem, recv_sem)

    def body(first, g, carry):
        operand = gather_group(scratch, g, devices, span, per_group, height)
        spectrum = jnp.dot(anal[g, first:, :], operand, preferred_element_type=F32).astype(BF16)
        scaled = (spectrum.astype(F32) * widen(filt, first, 2 * per_group)).astype(BF16)
        mixed = [
            jnp.dot(
                scaled[:, j * 256 : (j + 1) * 256], weight[...], preferred_element_type=F32
            ).astype(BF16)
            for j in range(per_group)
        ]
        mixed = mixed[0] if per_group == 1 else jnp.concatenate(mixed, 1)
        value = jnp.dot(tsynth[g, :, first:], mixed, preferred_element_type=F32)
        scatter_group(value, back, g, devices, span, per_group, height)
        return carry

    def after(q):
        pack(back, out, q)
        if q == 0:
            await_greetings(devices)
        exchange.send(q)

    over_groups(groups, sections, body, after)
    exchange.finish()


def backward_kernel(
    per_group, src, gsrc, anal, synth, tanal, filt, weight, received, total,
    out, scratch, gscratch, wgrad, fgrad, red, inbox, send_sem, recv_sem, rsend_sem, rrecv_sem,
):
    sections, devices, span, _ = src.shape
    groups, _, width = anal.shape
    height = width // per_group
    greet(devices)
    unpack(src, scratch)
    unpack(gsrc, gscratch)
    wgrad[...] = jnp.zeros_like(wgrad)
    fgrad[...] = jnp.zeros_like(fgrad)
    exchange = Exchange(out, received, send_sem, recv_sem)

    def body(first, g, carry):
        operand = gather_group(scratch, g, devices, span, per_group, height)
        goperand = gather_group(gscratch, g, devices, span, per_group, height)
        gain = widen(filt, first, 2)
        outs = []
        spectrum = jnp.dot(anal[g, first:, :], operand, preferred_element_type=F32).astype(BF16)
        gmixed = jnp.dot(synth[g, first:, :], goperand, preferred_element_type=F32).astype(BF16)
        for j in range(per_group):
            lanes = slice(j * 256, (j + 1) * 256)
            spec = spectrum[:, lanes].astype(F32)
            scaled = (spec * gain).astype(BF16)
            gmix = gmixed[:, lanes]
            wgrad[...] += lax.dot_general(
                scaled, gmix, (((0,), (0,)), ((), ())), preferred_element_type=F32
            )
            gscaled = lax.dot_general(
                gmix, weight[...], (((1,), (1,)), ((), ())), preferred_element_type=F32
            )
            term = gscaled * spec
            fgrad[first:, :] += term[:, :128] + term[:, 128:]
            outs.append((gscaled * gain).astype(BF16))
        gspectrum = outs[0] if per_group == 1 else jnp.concatenate(outs, 1)
        value = jnp.dot(tanal[g, :, first:], gspectrum, preferred_element_type=F32)
        scatter_group(value, scratch, g, devices, span, per_group, height)
        return carry

    def after(q):
        pack(scratch, out, q)
        if q == 0:
            await_greetings(devices)
        exchange.send(q)

    over_groups(groups, sections, body, after)
    half = wgrad.shape[0] // 2
    pieces = [
        (wgrad[:half, :half] + wgrad[half:, half:]) * (1.0 / MODES),
        (wgrad[:half, half:] - wgrad[half:, :half]) * (1.0 / MODES),
        fgrad[...] * 0.125,
    ]
    spare = red.shape[0] * red.shape[1] - 2 * half - MODES
    if spare:
        pieces.append(jnp.zeros((spare, 128), F32))
    red[...] = jnp.concatenate(pieces, 0).reshape(red.shape)
    reduce_all(red, inbox, total, rsend_sem, rrecv_sem)
    exchange.finish()


def gelu_slope(field):
    return 0.5 * (1.0 + lax.erf(field * (1.0 / math.sqrt(2.0)))) + field * jnp.exp(
        -0.5 * field * field
    ) * (1.0 / math.sqrt(2.0 * math.pi))


LON_CHUNK = 288


def merged(src):
    sections, devices, span, width = src.shape
    return src[...].astype(F32).reshape(sections * devices * span, width)


def slope_kernel(src, alpha, table, ttable, upstream, received, out, slope, send_sem, recv_sem):
    lat_local, lon_count, channels = upstream.shape
    sections, devices = out.shape[:2]
    greet(devices)
    operand = (merged(src) * alpha[:, 0:1]).astype(BF16)

    def grid_rows(q, carry):
        rows = pl.ds(pl.multiple_of(q * LON_CHUNK, LON_CHUNK), LON_CHUNK)
        field = jnp.dot(ttable[rows, :], operand, preferred_element_type=F32)
        up = jnp.concatenate([upstream[a, rows, :] for a in range(lat_local)], 1)
        slope[rows, :] = (up.astype(F32) * gelu_slope(field)).astype(BF16)
        return carry

    lax.fori_loop(0, lon_count // LON_CHUNK, grid_rows, 0)
    await_greetings(devices)
    exchange = Exchange(out, received, send_sem, recv_sem)
    for section in range(sections):
        section_product(table, slope[...], out, section, alpha)
        exchange.send(section)
    exchange.finish()


def final_kernel(src, ttable, upstream, out):
    lat_local, lon_count, channels = upstream.shape
    operand = merged(src).astype(BF16)

    def grid_rows(q, carry):
        rows = pl.ds(pl.multiple_of(q * LON_CHUNK, LON_CHUNK), LON_CHUNK)
        value = jnp.dot(ttable[rows, :], operand, preferred_element_type=F32)
        for a in range(lat_local):
            part = value[:, a * channels : (a + 1) * channels]
            out[a, rows, :] = (part + upstream[a, rows, :].astype(F32)).astype(BF16)
        return carry

    lax.fori_loop(0, lon_count // LON_CHUNK, grid_rows, 0)


def mixing_matrix(mix_weight):
    upper = jnp.concatenate([mix_weight[0], mix_weight[1]], 1)
    lower = jnp.concatenate([-mix_weight[1], mix_weight[0]], 1)
    return jnp.concatenate([upper, lower], 0)


def shape(dims, kind=BF16):
    return jax.ShapeDtypeStruct(dims, kind)


def body(grid_in, upstream, mix_weight, degree_filter):
    devices = lax.axis_size("space")
    me = lax.axis_index("space")
    lat_local, lon_count, channels = grid_in.shape
    lat_count = lat_local * devices
    slots = MODES // devices
    sections = sections_of(devices)
    span = 2 * slots // sections
    height = 64 if lat_count <= 64 else -(-lat_count // 128) * 128
    per_group = 128 // height if height < 128 else 1
    width = height * per_group
    groups = slots // per_group
    dims = (sections, devices, span, lat_local * channels)
    packet = shape(dims)
    outgoing = pltpu.VMEM(dims, BF16)
    semaphores = pltpu.SemaphoreType.DMA((sections, devices))

    lane = jnp.arange(width, dtype=jnp.int32)
    within = lane % height
    valid = within < lat_count
    latitude = jnp.where(valid, within % devices * lat_local + within // devices, 0)
    angles = latitude_angles(latitude, lat_count)
    group = jnp.minimum(jnp.arange(-(-groups // 8) * 8, dtype=jnp.int32), groups - 1)[:, None]
    orders = ((group * per_group + lane[None, :] // height) * devices + me).astype(F32)
    cosine = jnp.broadcast_to(jnp.cos(angles)[None, :], orders.shape)
    start = 0.5 * (jnp.log(2.0 * orders + 1.0) - math.log(2.0))
    start = start + 0.5 * (
        lax.lgamma(2.0 * orders + 1.0) - 2.0 * lax.lgamma(orders + 1.0) - orders * math.log(4.0)
    )
    start = start + orders * jnp.log(jnp.sin(angles))[None, :]
    weights = jnp.where(valid, math.pi / lat_count * jnp.sin(angles), 0.0)
    tall = shape((groups, MODES, width))
    flat = shape((groups, width, MODES))
    table, ttable, spectral_in, synth, anal, tsynth, tanal = pl.pallas_call(
        fourier_kernel,
        out_shape=(
            shape((2 * MODES, lon_count)),
            shape((lon_count, 2 * MODES)),
            packet,
            tall,
            tall,
            flat,
            flat,
        ),
        scratch_shapes=[
            outgoing,
            pltpu.VMEM((width // 128, MODES * orders.shape[0], 128), F32),
            semaphores,
            semaphores,
        ],
        compiler_params=params(collective_id=0, has_side_effects=True),
        name="fourier_stage",
    )(
        *base_tables(devices, lon_count),
        grid_in,
        orders,
        cosine,
        start,
        jnp.broadcast_to(weights[None, :], (8, width)),
        jnp.broadcast_to(weights[:, None], (width, 128)),
    )

    wide_weight = mixing_matrix(mix_weight)
    slab = pltpu.VMEM((lat_local, 2 * MODES, 128), F32)
    returned = pl.pallas_call(
        functools.partial(forward_kernel, per_group),
        out_shape=packet,
        scratch_shapes=[outgoing, slab, slab, semaphores, semaphores],
        compiler_params=params(collective_id=1, has_side_effects=True),
        name="forward_stage",
    )(spectral_in, anal, tsynth, degree_filter, wide_weight)

    order, _ = row_phase(jnp.arange(2 * MODES, dtype=jnp.int32), devices, lon_count)
    alpha = jnp.broadcast_to(jnp.where(order == 0, 1.0, 2.0).astype(F32)[:, None], (2 * MODES, 128))
    gradient_in = pl.pallas_call(
        slope_kernel,
        out_shape=packet,
        scratch_shapes=[
            outgoing,
            pltpu.VMEM((lon_count, lat_local * channels), BF16),
            semaphores,
            semaphores,
        ],
        compiler_params=params(collective_id=2, has_side_effects=True),
        name="slope_stage",
    )(returned, alpha, table, ttable, upstream)

    share = -(-(2 * channels + MODES) // (8 * devices)) * 8
    blocks = (devices, share, channels)
    hops = pltpu.SemaphoreType.DMA((2 * devices.bit_length(),))
    gfield, summed = pl.pallas_call(
        functools.partial(backward_kernel, per_group),
        out_shape=(packet, shape(blocks, F32)),
        scratch_shapes=[
            outgoing,
            slab,
            slab,
            pltpu.VMEM((2 * channels, 2 * channels), F32),
            pltpu.VMEM((MODES, channels), F32),
            pltpu.VMEM(blocks, F32),
            pltpu.VMEM(blocks, F32),
            semaphores,
            semaphores,
            hops,
            hops,
        ],
        compiler_params=params(collective_id=3, has_side_effects=True),
        name="backward_stage",
    )(spectral_in, gradient_in, anal, synth, tanal, degree_filter, wide_weight)
    summed = summed.reshape(devices * share, channels)

    grad_in = pl.pallas_call(
        final_kernel,
        out_shape=shape(grid_in.shape),
        compiler_params=params(),
        name="final_stage",
    )(gfield, ttable, upstream)
    return (
        grad_in,
        summed[: 2 * channels].reshape(2, channels, channels),
        summed[2 * channels : 2 * channels + MODES],
    )


def solution(mesh):
    return jax.shard_map(
        body,
        mesh=mesh,
        in_specs=(P(("groups", "space"), None, None), P(("groups", "space"), None, None), P(), P()),
        out_specs=(P(("groups", "space"), None, None), P("groups", None, None), P("groups", None)),
        check_vma=False,
    )
```

```python
import functools
import math

import jax
import jax.numpy as jnp
import numpy as np
from jax import lax
from jax.experimental import pallas as pl
from jax.experimental.pallas import tpu as pltpu
from jax.sharding import PartitionSpec as P

MODES = 512
ROWS = 32
F32 = jnp.float32
BF16 = jnp.bfloat16


def params(**extra):
    return pltpu.CompilerParams(vmem_limit_bytes=56 * 1024 * 1024, **extra)


def latitude_angles(index, lat_count):
    return math.pi * (index.astype(F32) + 0.5) / lat_count


def greet(devices):
    me = lax.axis_index("space")
    barrier = pltpu.get_barrier_semaphore()

    def hello(step, carry):
        peer = (me + step) % devices
        pl.semaphore_signal(
            barrier, inc=1, device_id={"space": peer}, device_id_type=pl.DeviceIdType.MESH
        )
        return carry

    lax.fori_loop(1, devices, hello, 0)


def await_greetings(devices):
    pl.semaphore_wait(pltpu.get_barrier_semaphore(), devices - 1)


def remote(src, dst, send_sem, recv_sem, peer):
    return pltpu.make_async_remote_copy(
        src_ref=src,
        dst_ref=dst,
        send_sem=send_sem,
        recv_sem=recv_sem,
        device_id={"space": peer},
        device_id_type=pl.DeviceIdType.MESH,
    )


class Exchange:
    def __init__(self, source, target, send_sem, recv_sem):
        self.source, self.target = source, target
        self.send_sem, self.recv_sem = send_sem, recv_sem
        self.devices = source.shape[1]
        self.me = lax.axis_index("space")

    def copy(self, section, step):
        peer = (self.me + step) % self.devices
        return remote(
            self.source.at[section, peer],
            self.target.at[section, self.me],
            self.send_sem.at[section, step],
            self.recv_sem.at[section, step],
            peer,
        )

    def send(self, section):
        half = self.devices // 2

        def one(index, carry):
            sign = 1 - 2 * (index % 2)
            step = (half + sign * ((index + 1) // 2) + self.devices) % self.devices
            self.copy(section, step).start()
            return carry

        lax.fori_loop(0, self.devices - 1, one, 0)
        self.target[section, self.me] = self.source[section, self.me]

    def arrive(self, section):
        def one(step, carry):
            self.copy(section, step).wait_recv()
            return carry

        lax.fori_loop(1, self.devices, one, 0)

    def drain(self):
        for section in range(self.source.shape[0]):

            def one(step, carry, section=section):
                self.copy(section, step).wait_send()
                return carry

            lax.fori_loop(1, self.devices, one, 0)


class Reduction:
    def __init__(self, red, inbox, total, send_sem, recv_sem):
        self.red, self.inbox, self.total = red, inbox, total
        self.send_sem, self.recv_sem = send_sem, recv_sem
        devices = red.shape[0]
        me = lax.axis_index("space")
        self.hops = []
        base = me * 0
        stride = 1
        while stride < devices:
            half = devices // (2 * stride)
            bit = me // stride % 2
            keep, give = base + bit * half, base + (1 - bit) * half
            self.hops.append((half, keep, give, me + (1 - 2 * bit) * stride))
            base = keep
            stride *= 2
        self.base = base

    def scatter(self):
        for t, (half, keep, give, partner) in enumerate(self.hops):
            copy = remote(
                self.red.at[pl.ds(give, half)],
                self.inbox.at[pl.ds(half, half)],
                self.send_sem.at[t],
                self.recv_sem.at[t],
                partner,
            )
            copy.start()
            copy.wait()
            self.red[pl.ds(keep, half)] += self.inbox[half : 2 * half]
        self.total[pl.ds(self.base, 1)] = self.red[pl.ds(self.base, 1)]

    def gather(self, index):
        count = len(self.hops)
        t = count - 1 - index
        half, keep, _, partner = self.hops[t]
        block = self.total.at[pl.ds(keep, half)]
        copy = remote(
            block, block, self.send_sem.at[count + t], self.recv_sem.at[count + t], partner
        )
        copy.start()
        return copy


def sections_of(devices):
    return max(1, min(4, MODES // devices // 8))


def row_phase(rows, devices, lon_count):
    span = 2 * MODES // devices // sections_of(devices)
    section = rows // (span * devices)
    device = rows // span % devices
    part = rows // (span // 2) % 2
    slot = section * (span // 2) + rows % (span // 2)
    return slot * devices + device, part * (lon_count // 4)


def cosine_of(phase, lon_count):
    turn = phase - jnp.floor(phase * (1.0 / lon_count)) * lon_count
    x = (lon_count / 4 - jnp.abs(turn - lon_count / 2)) * (2.0 * math.pi / lon_count)
    y = x * x
    tail = 1.0 / 362880.0 - y * (1.0 / 39916800.0)
    tail = 1.0 / 120.0 + y * (-1.0 / 5040.0 + y * tail)
    return -x * (1.0 + y * (-1.0 / 6.0 + y * tail))


def angle_indices(devices, lon_count):
    order, offset = row_phase(np.arange(2 * MODES), devices, lon_count)

    def column(values):
        return np.broadcast_to(values.astype(np.float32)[:, None], (len(values), 128))

    def lanes(values):
        return np.broadcast_to(values.astype(np.float32)[None, :], (8, len(values)))

    columns = np.stack([column(v) for v in (order[::ROWS], offset[::ROWS], order[:ROWS], offset[:ROWS])])
    return jnp.asarray(columns), jnp.asarray(np.stack([lanes(order), lanes(offset)]))


def angles_by_row(columns, lon_count, big, small):
    rows = big.shape[1]
    lon = lax.broadcasted_iota(jnp.int32, (rows, lon_count), 1).astype(F32)
    phase = columns[0][:, 0:1] * lon + columns[1][:, 0:1]
    big[0] = cosine_of(phase, lon_count)
    big[1] = cosine_of(phase + 0.75 * lon_count, lon_count)
    lon = lax.broadcasted_iota(jnp.int32, (ROWS, lon_count), 1).astype(F32)
    phase = columns[2][:, 0:1] * lon + columns[3][:, 0:1]
    factor = 1.0 / math.sqrt(lon_count)
    small[0] = cosine_of(phase, lon_count) * factor
    small[1] = cosine_of(phase + 0.75 * lon_count, lon_count) * factor


def angles_by_lane(lanes, lon_count, big, small):
    rows, total = big.shape[1:]
    order, offset = lanes[0, 0:1, :], lanes[1, 0:1, :]
    lon = lax.broadcasted_iota(jnp.int32, (rows, total), 0).astype(F32) * float(ROWS)
    phase = lon * order
    big[0] = cosine_of(phase, lon_count)
    big[1] = cosine_of(phase + 0.75 * lon_count, lon_count)
    lon = lax.broadcasted_iota(jnp.int32, (ROWS, total), 0).astype(F32)
    phase = lon * order + offset
    factor = 1.0 / math.sqrt(lon_count)
    small[0] = cosine_of(phase, lon_count) * factor
    small[1] = cosine_of(phase + 0.75 * lon_count, lon_count) * factor


def fill(dst, big, small, count):
    def step(h, carry):
        value = big[0, pl.ds(h, 1), :] * small[0] - big[1, pl.ds(h, 1), :] * small[1]
        dst[pl.ds(pl.multiple_of(h * ROWS, ROWS), ROWS), :] = value.astype(BF16)
        return carry

    lax.fori_loop(0, count, step, 0)


def alpha_column(section, rows, span):
    row = lax.broadcasted_iota(jnp.int32, (rows, 128), 0)
    zero = jnp.logical_or(row == 0, row == span // 2)
    alpha = jnp.where(zero, 1.0, 2.0) if section == 0 else jnp.full((rows, 128), 2.0, F32)
    return alpha[:, 0:1]


def section_product(table, wide, out, section, scaled):
    _, devices, span, width = out.shape
    count = devices * span
    chunk = 256
    each = chunk // span
    for q in range(count // chunk):
        first = section * count + q * chunk
        value = jnp.dot(table[first : first + chunk, :], wide, preferred_element_type=F32)
        if scaled:
            value = value * (alpha_column(0, chunk, span) if first == 0 else 2.0)
        out[section, q * each : (q + 1) * each] = value.astype(BF16).reshape(each, span, width)


def legendre_tables(
    slot_ref, start_ref, lat_ref, synth, anal, tsynth, tanal, hold
):
    groups, width = slot_ref.shape
    orders = slot_ref[...] + lax.axis_index("space").astype(F32)
    order_sq = orders * orders
    cosine = lat_ref[0:1, :]
    wrow = lat_ref[1:2, :]
    wcol = jnp.broadcast_to(wrow, (128, width)).T[:, 0:1]
    block = 32

    def degree_block(index, carry):
        p_now, p_prev, e_prev, log_scale = carry
        scale = jnp.exp(log_scale)
        base = index * block
        for inner in range(block):
            degree_int = base + inner
            degree = degree_int.astype(F32)
            active = degree > orders
            square = degree * degree
            ratio = jnp.maximum(square - order_sq, 1.0) / jnp.maximum(4.0 * square - 1.0, 1.0)
            coef = lax.rsqrt(ratio)
            p_next = jnp.where(active, coef * (cosine * p_now - e_prev * p_prev), p_now)
            p_prev = jnp.where(active, p_now, p_prev)
            e_prev = jnp.where(active, ratio * coef, 0.0)
            p_now = p_next
            value = jnp.where(degree >= orders, p_now * scale, 0.0)
            rows = pl.ds(pl.multiple_of(degree_int * groups, groups), groups)
            for part in range(width // 128):
                hold[part, rows, :] = value[:, part * 128 : (part + 1) * 128]
        magnitude = jnp.maximum(jnp.abs(p_now), jnp.abs(p_prev))
        return (p_now / magnitude, p_prev / magnitude, e_prev, log_scale + jnp.log(magnitude))

    ones = jnp.ones((groups, width), F32)
    zeros = jnp.zeros((groups, width), F32)
    lax.fori_loop(0, MODES // block, degree_block, (ones, zeros, zeros, start_ref[...]))

    def spread(g, carry):
        pieces = [
            hold[part, pl.ds(g, MODES, stride=groups), :]
            for part in range(width // 128)
        ]
        value = pieces[0] if len(pieces) == 1 else jnp.concatenate(pieces, 1)
        synth[g] = value.astype(BF16)
        anal[g] = (value * wrow).astype(BF16)
        turned = value.T
        tsynth[g] = turned.astype(BF16)
        tanal[g] = (turned * wcol).astype(BF16)
        return carry

    lax.fori_loop(0, synth.shape[0], spread, 0)


def unpack(src, scratch, q):
    _, devices, span, _ = src.shape
    for a in range(scratch.shape[0]):
        part = src[q, :, :, a * 128 : (a + 1) * 128].astype(F32)
        scratch[a, q * devices * span : (q + 1) * devices * span] = part.reshape(devices * span, 128)


def pack(scratch, dst, q):
    _, devices, span, _ = dst.shape
    for a in range(scratch.shape[0]):
        part = scratch[a, q * devices * span : (q + 1) * devices * span]
        dst[q, :, :, a * 128 : (a + 1) * 128] = part.reshape(devices, span, 128).astype(BF16)


def strided_rows(s, r, devices, span):
    half = span // 2
    start = s // half * (devices * span) + r * half + s % half
    return pl.ds(start, devices, stride=span)


def gather_group(scratch, g, devices, span, per_group, height):
    lat_local = scratch.shape[0]
    rows = []
    for j in range(per_group):
        s = g * per_group + j
        halves = []
        for r in range(2):
            pick = strided_rows(s, r, devices, span)
            parts = [scratch[a, pick, :] for a in range(lat_local)]
            if height > devices * lat_local:
                parts.append(jnp.zeros((height - devices * lat_local, 128), F32))
            halves.append(jnp.concatenate(parts, 0))
        zero = jnp.zeros((height, 256), F32)
        cells = [zero] * per_group
        cells[j] = jnp.concatenate(halves, 1)
        rows.append(cells[0] if per_group == 1 else jnp.concatenate(cells, 1))
    return (rows[0] if per_group == 1 else jnp.concatenate(rows, 0)).astype(BF16)


def scatter_group(value, scratch, g, devices, span, per_group, height):
    lat_local = scratch.shape[0]
    for j in range(per_group):
        s = g * per_group + j
        for r in range(2):
            for a in range(lat_local):
                top = j * height + a * devices
                left = j * 256 + r * 128
                scratch[a, strided_rows(s, r, devices, span), :] = value[
                    top : top + devices, left : left + 128
                ]


def over_groups(groups, sections, section, body):
    pieces = 4
    each = groups // pieces
    share = pieces // sections
    for q in range(section * share, (section + 1) * share):
        first = q * (MODES // pieces)
        lax.fori_loop(q * each, (q + 1) * each, functools.partial(body, first), 0)


def widen(filter_ref, first, copies):
    gain = filter_ref[first:, :].astype(F32)
    return jnp.concatenate([gain] * copies, 1)


def forward_body(per_group, shapes, anal, tsynth, filt, weight, scratch, back):
    _, devices, span, _ = shapes
    height = anal.shape[2] // per_group

    def body(first, g, carry):
        operand = gather_group(scratch, g, devices, span, per_group, height)
        spectrum = jnp.dot(anal[g, first:, :], operand, preferred_element_type=F32).astype(BF16)
        scaled = (spectrum.astype(F32) * widen(filt, first, 2 * per_group)).astype(BF16)
        mixed = [
            jnp.dot(
                scaled[:, j * 256 : (j + 1) * 256], weight[...], preferred_element_type=F32
            ).astype(BF16)
            for j in range(per_group)
        ]
        mixed = mixed[0] if per_group == 1 else jnp.concatenate(mixed, 1)
        value = jnp.dot(tsynth[g, :, first:], mixed, preferred_element_type=F32)
        scatter_group(value, back, g, devices, span, per_group, height)
        return carry

    return body


def backward_body(
    per_group, shapes, anal, synth, tanal, filt, weight, scratch, gscratch, wgrad, fgrad
):
    _, devices, span, _ = shapes
    height = anal.shape[2] // per_group

    def body(first, g, carry):
        operand = gather_group(scratch, g, devices, span, per_group, height)
        goperand = gather_group(gscratch, g, devices, span, per_group, height)
        gain = widen(filt, first, 2)
        outs = []
        spectrum = jnp.dot(anal[g, first:, :], operand, preferred_element_type=F32).astype(BF16)
        gmixed = jnp.dot(synth[g, first:, :], goperand, preferred_element_type=F32).astype(BF16)
        for j in range(per_group):
            lanes = slice(j * 256, (j + 1) * 256)
            spec = spectrum[:, lanes].astype(F32)
            scaled = (spec * gain).astype(BF16)
            gmix = gmixed[:, lanes]
            wgrad[...] += lax.dot_general(
                scaled, gmix, (((0,), (0,)), ((), ())), preferred_element_type=F32
            )
            gscaled = lax.dot_general(
                gmix, weight[...], (((1,), (1,)), ((), ())), preferred_element_type=F32
            )
            term = gscaled * spec
            fgrad[first:, :] += term[:, :128] + term[:, 128:]
            outs.append((gscaled * gain).astype(BF16))
        gspectrum = outs[0] if per_group == 1 else jnp.concatenate(outs, 1)
        value = jnp.dot(tanal[g, :, first:], gspectrum, preferred_element_type=F32)
        scatter_group(value, scratch, g, devices, span, per_group, height)
        return carry

    return body


def fold_gradients(wgrad, fgrad, red):
    half = wgrad.shape[0] // 2
    pieces = [
        (wgrad[:half, :half] + wgrad[half:, half:]) * (1.0 / MODES),
        (wgrad[:half, half:] - wgrad[half:, :half]) * (1.0 / MODES),
        fgrad[...] * 0.125,
    ]
    spare = red.shape[0] * red.shape[1] - 2 * half - MODES
    if spare:
        pieces.append(jnp.zeros((spare, 128), F32))
    red[...] = jnp.concatenate(pieces, 0).reshape(red.shape)


def gelu_slope(field):
    return 0.5 * (1.0 + lax.erf(field * (1.0 / math.sqrt(2.0)))) + field * jnp.exp(
        -0.5 * field * field
    ) * (1.0 / math.sqrt(2.0 * math.pi))


LON_CHUNK = 288


def merged(src, section):
    _, devices, span, width = src.shape
    return src[section].astype(F32).reshape(devices * span, width)


def add_section(ttable, operand, section, field, last):
    count = operand.shape[0]
    lon_count = field.shape[0]

    def grid_rows(q, carry):
        rows = pl.ds(pl.multiple_of(q * LON_CHUNK, LON_CHUNK), LON_CHUNK)
        value = jnp.dot(
            ttable[rows, section * count : (section + 1) * count],
            operand,
            preferred_element_type=F32,
        )
        if section:
            value = value + field[rows, :]
        if last is None:
            field[rows, :] = value
        else:
            last(rows, value)
        return carry

    lax.fori_loop(0, lon_count // LON_CHUNK, grid_rows, 0)


def block_kernel(
    per_group,
    columns, lanes, grid, upstream, slots, start, lats, filt, weight,
    grad, total,
    table, ttable, big, small, tbig, tsmall,
    synth, anal, tsynth, tanal, hold,
    out1, in1, out2, in2, out3, in3, out4, in4,
    scratch, back, field, slope, wgrad, fgrad, red, inbox,
    send1, recv1, send2, recv2, send3, recv3, send4, recv4, rsend, rrecv,
):
    shapes = out1.shape
    sections, devices, span, _ = shapes
    lat_local, lon_count, channels = grid.shape
    groups = synth.shape[0]
    greet(devices)
    angles_by_row(columns, lon_count, big, small)
    fill(table, big, small, big.shape[1])

    first = Exchange(out1, in1, send1, recv1)
    wide = jnp.concatenate([grid[a] for a in range(lat_local)], 1)
    for q in range(sections):
        section_product(table, wide, out1, q, False)
        if q == 0:
            await_greetings(devices)
        first.send(q)
    legendre_tables(slots, start, lats, synth, anal, tsynth, tanal, hold)
    angles_by_lane(lanes, lon_count, tbig, tsmall)
    fill(ttable, tbig, tsmall, tbig.shape[1])

    second = Exchange(out2, in2, send2, recv2)
    forward = forward_body(per_group, shapes, anal, tsynth, filt, weight, scratch, back)
    for q in range(sections):
        first.arrive(q)
        unpack(in1, scratch, q)
        over_groups(groups, sections, q, forward)
        pack(back, out2, q)
        second.send(q)

    def gate(rows, value):
        up = jnp.concatenate([upstream[a, rows, :] for a in range(lat_local)], 1)
        slope[rows, :] = (up.astype(F32) * gelu_slope(value)).astype(BF16)

    for q in range(sections):
        second.arrive(q)
        operand = merged(in2, q)
        operand = (operand * alpha_column(q, operand.shape[0], span)).astype(BF16)
        add_section(ttable, operand, q, field, gate if q == sections - 1 else None)

    third = Exchange(out3, in3, send3, recv3)
    for q in range(sections):
        section_product(table, slope[...], out3, q, True)
        third.send(q)

    wgrad[...] = jnp.zeros_like(wgrad)
    fgrad[...] = jnp.zeros_like(fgrad)
    fourth = Exchange(out4, in4, send4, recv4)
    backward = backward_body(
        per_group, shapes, anal, synth, tanal, filt, weight, scratch, back, wgrad, fgrad
    )
    for q in range(sections):
        third.arrive(q)
        unpack(in3, back, q)
        over_groups(groups, sections, q, backward)
        pack(scratch, out4, q)
        if q < sections - 1:
            fourth.send(q)
    fold_gradients(wgrad, fgrad, red)
    reduction = Reduction(red, inbox, total, rsend, rrecv)
    reduction.scatter()
    fourth.send(sections - 1)

    def finish(rows, value):
        for a in range(lat_local):
            part = value[:, a * channels : (a + 1) * channels]
            grad[a, rows, :] = (part + upstream[a, rows, :].astype(F32)).astype(BF16)

    hops = len(reduction.hops)
    for step in range(max(hops, sections)):
        copy = reduction.gather(step) if step < hops else None
        if step < sections:
            fourth.arrive(step)
            add_section(
                ttable,
                merged(in4, step).astype(BF16),
                step,
                field,
                finish if step == sections - 1 else None,
            )
        if copy is not None:
            copy.wait()
    for exchange in (first, second, third, fourth):
        exchange.drain()


def mixing_matrix(mix_weight):
    upper = jnp.concatenate([mix_weight[0], mix_weight[1]], 1)
    lower = jnp.concatenate([-mix_weight[1], mix_weight[0]], 1)
    return jnp.concatenate([upper, lower], 0)


def body(grid_in, upstream, mix_weight, degree_filter):
    devices = lax.axis_size("space")
    me = lax.axis_index("space")
    lat_local, lon_count, channels = grid_in.shape
    lat_count = lat_local * devices
    slots = MODES // devices
    sections = sections_of(devices)
    span = 2 * slots // sections
    height = 64 if lat_count <= 64 else -(-lat_count // 128) * 128
    per_group = 128 // height if height < 128 else 1
    width = height * per_group
    groups = slots // per_group
    dims = (sections, devices, span, lat_local * channels)

    lane = np.arange(width)
    within = lane % height
    valid = within < lat_count
    latitude = np.where(valid, within % devices * lat_local + within // devices, 0)
    padded = -(-groups // 8) * 8
    group = np.minimum(np.arange(padded), groups - 1)[:, None]
    slot_orders = ((group * per_group + lane[None, :] // height) * devices).astype(np.float32)
    slot_orders = jnp.asarray(slot_orders)
    angles = latitude_angles(jnp.asarray(latitude), lat_count)
    orders = slot_orders + me.astype(F32)
    start = 0.5 * (jnp.log(2.0 * orders + 1.0) - math.log(2.0))
    start = start + 0.5 * (
        lax.lgamma(2.0 * orders + 1.0) - 2.0 * lax.lgamma(orders + 1.0) - orders * math.log(4.0)
    )
    start = start + orders * jnp.log(jnp.sin(angles))[None, :]
    row = jnp.arange(8)[:, None]
    weights = math.pi / lat_count * jnp.sin(angles) * jnp.asarray(valid.astype(np.float32))
    lats = jnp.where(row == 0, jnp.cos(angles)[None, :], weights[None, :])

    share = -(-(2 * channels + MODES) // (8 * devices)) * 8
    blocks = (devices, share, channels)
    vmem = pltpu.VMEM
    slab = vmem((lat_local, 2 * MODES, 128), F32)
    total_rows = 2 * MODES
    semaphores = pltpu.SemaphoreType.DMA((sections, devices))
    hops = pltpu.SemaphoreType.DMA((2 * devices.bit_length(),))
    grad_in, summed = pl.pallas_call(
        functools.partial(block_kernel, per_group),
        out_shape=(
            jax.ShapeDtypeStruct(grid_in.shape, BF16),
            jax.ShapeDtypeStruct(blocks, F32),
        ),
        scratch_shapes=[
            vmem((total_rows, lon_count), BF16),
            vmem((lon_count, total_rows), BF16),
            vmem((2, total_rows // ROWS, lon_count), F32),
            vmem((2, ROWS, lon_count), F32),
            vmem((2, lon_count // ROWS, total_rows), F32),
            vmem((2, ROWS, total_rows), F32),
            vmem((groups, MODES, width), BF16),
            vmem((groups, MODES, width), BF16),
            vmem((groups, width, MODES), BF16),
            vmem((groups, width, MODES), BF16),
            vmem((width // 128, MODES * padded, 128), F32),
            *[vmem(dims, BF16)] * 8,
            slab,
            slab,
            vmem((lon_count, lat_local * channels), F32),
            vmem((lon_count, lat_local * channels), BF16),
            vmem((2 * channels, 2 * channels), F32),
            vmem((MODES, channels), F32),
            vmem(blocks, F32),
            vmem(blocks, F32),
            *[semaphores] * 8,
            hops,
            hops,
        ],
        compiler_params=params(collective_id=0, has_side_effects=True),
        name="block",
    )(
        *angle_indices(devices, lon_count),
        grid_in,
        upstream,
        slot_orders,
        start,
        lats,
        degree_filter,
        mixing_matrix(mix_weight),
    )
    summed = summed.reshape(devices * share, channels)
    return (
        grad_in,
        summed[: 2 * channels].reshape(2, channels, channels),
        summed[2 * channels : 2 * channels + MODES],
    )


def solution(mesh):
    return jax.shard_map(
        body,
        mesh=mesh,
        in_specs=(P(("groups", "space"), None, None), P(("groups", "space"), None, None), P(), P()),
        out_specs=(P(("groups", "space"), None, None), P("groups", None, None), P("groups", None)),
        check_vma=False,
    )
```

```python
import functools
import math

import jax
import jax.numpy as jnp
import numpy as np
from jax import lax
from jax.experimental import pallas as pl
from jax.experimental.pallas import tpu as pltpu
from jax.sharding import PartitionSpec as P

MODES = 512
ROWS = 32
F32 = jnp.float32
BF16 = jnp.bfloat16


def params(**extra):
    return pltpu.CompilerParams(vmem_limit_bytes=56 * 1024 * 1024, **extra)


def latitude_angles(index, lat_count):
    return math.pi * (index.astype(F32) + 0.5) / lat_count


def greet(devices):
    me = lax.axis_index("space")
    barrier = pltpu.get_barrier_semaphore()

    def hello(step, carry):
        peer = (me + step) % devices
        pl.semaphore_signal(
            barrier, inc=1, device_id={"space": peer}, device_id_type=pl.DeviceIdType.MESH
        )
        return carry

    lax.fori_loop(1, devices, hello, 0)


def await_greetings(devices):
    pl.semaphore_wait(pltpu.get_barrier_semaphore(), devices - 1)


def remote(src, dst, send_sem, recv_sem, peer):
    return pltpu.make_async_remote_copy(
        src_ref=src,
        dst_ref=dst,
        send_sem=send_sem,
        recv_sem=recv_sem,
        device_id={"space": peer},
        device_id_type=pl.DeviceIdType.MESH,
    )


class Exchange:
    def __init__(self, source, target, send_sem, recv_sem):
        self.source, self.target = source, target
        self.send_sem, self.recv_sem = send_sem, recv_sem
        self.devices = source.shape[1]
        self.me = lax.axis_index("space")

    def copy(self, section, step):
        peer = (self.me + step) % self.devices
        return remote(
            self.source.at[section, peer],
            self.target.at[section, self.me],
            self.send_sem.at[section, step],
            self.recv_sem.at[section, step],
            peer,
        )

    def send(self, section):
        half = self.devices // 2

        def one(index, carry):
            sign = 1 - 2 * (index % 2)
            step = (half + sign * ((index + 1) // 2) + self.devices) % self.devices
            self.copy(section, step).start()
            return carry

        lax.fori_loop(0, self.devices - 1, one, 0)
        self.target[section, self.me] = self.source[section, self.me]

    def arrive(self, section):
        def one(step, carry):
            self.copy(section, step).wait_recv()
            return carry

        lax.fori_loop(1, self.devices, one, 0)

    def drain(self):
        for section in range(self.source.shape[0]):

            def one(step, carry, section=section):
                self.copy(section, step).wait_send()
                return carry

            lax.fori_loop(1, self.devices, one, 0)


class Reduction:
    def __init__(self, red, inbox, total, send_sem, recv_sem):
        self.red, self.inbox, self.total = red, inbox, total
        self.send_sem, self.recv_sem = send_sem, recv_sem
        devices = red.shape[0]
        me = lax.axis_index("space")
        self.hops = []
        base = me * 0
        stride = 1
        while stride < devices:
            half = devices // (2 * stride)
            bit = me // stride % 2
            keep, give = base + bit * half, base + (1 - bit) * half
            self.hops.append((half, keep, give, me + (1 - 2 * bit) * stride))
            base = keep
            stride *= 2
        self.base = base

    def scatter(self, held):
        count = len(self.hops)
        early = max(1, len(held) - 2) if held else 0
        for send in held[:early]:
            send()
        late = held[early:]
        for t, (half, keep, give, partner) in enumerate(self.hops):
            copy = remote(
                self.red.at[pl.ds(give, half)],
                self.inbox.at[pl.ds(half, half)],
                self.send_sem.at[t],
                self.recv_sem.at[t],
                partner,
            )
            copy.start()
            index = t - (count - len(late))
            if index >= 0:
                late[index]()
            copy.wait()
            self.red[pl.ds(keep, half)] += self.inbox[half : 2 * half]
        self.total[pl.ds(self.base, 1)] = self.red[pl.ds(self.base, 1)]

    def gather(self, index):
        count = len(self.hops)
        t = count - 1 - index
        half, keep, _, partner = self.hops[t]
        block = self.total.at[pl.ds(keep, half)]
        copy = remote(
            block, block, self.send_sem.at[count + t], self.recv_sem.at[count + t], partner
        )
        copy.start()
        return copy


def sections_of(devices):
    return max(1, min(4, MODES // devices // 8))


def row_phase(rows, devices, lon_count):
    span = 2 * MODES // devices // sections_of(devices)
    section = rows // (span * devices)
    device = rows // span % devices
    part = rows // (span // 2) % 2
    slot = section * (span // 2) + rows % (span // 2)
    return slot * devices + device, part * (lon_count // 4)


def cosine_of(phase, lon_count):
    turn = phase - jnp.floor(phase * (1.0 / lon_count)) * lon_count
    x = (lon_count / 4 - jnp.abs(turn - lon_count / 2)) * (2.0 * math.pi / lon_count)
    y = x * x
    tail = 1.0 / 362880.0 - y * (1.0 / 39916800.0)
    tail = 1.0 / 120.0 + y * (-1.0 / 5040.0 + y * tail)
    return -x * (1.0 + y * (-1.0 / 6.0 + y * tail))


def angle_indices(devices, lon_count):
    order, offset = row_phase(np.arange(2 * MODES), devices, lon_count)

    def column(values):
        return np.broadcast_to(values.astype(np.float32)[:, None], (len(values), 128))

    def lanes(values):
        return np.broadcast_to(values.astype(np.float32)[None, :], (8, len(values)))

    columns = np.stack([column(v) for v in (order[::ROWS], offset[::ROWS], order[:ROWS], offset[:ROWS])])
    return jnp.asarray(columns), jnp.asarray(np.stack([lanes(order), lanes(offset)]))


def angles_by_row(columns, lon_count, big, small):
    rows = big.shape[1]
    lon = lax.broadcasted_iota(jnp.int32, (rows, lon_count), 1).astype(F32)
    phase = columns[0][:, 0:1] * lon + columns[1][:, 0:1]
    big[0] = cosine_of(phase, lon_count)
    big[1] = cosine_of(phase + 0.75 * lon_count, lon_count)
    lon = lax.broadcasted_iota(jnp.int32, (ROWS, lon_count), 1).astype(F32)
    phase = columns[2][:, 0:1] * lon + columns[3][:, 0:1]
    factor = 1.0 / math.sqrt(lon_count)
    small[0] = cosine_of(phase, lon_count) * factor
    small[1] = cosine_of(phase + 0.75 * lon_count, lon_count) * factor


def angles_by_lane(lanes, lon_count, big, small):
    rows, total = big.shape[1:]
    order, offset = lanes[0, 0:1, :], lanes[1, 0:1, :]
    lon = lax.broadcasted_iota(jnp.int32, (rows, total), 0).astype(F32) * float(ROWS)
    phase = lon * order
    big[0] = cosine_of(phase, lon_count)
    big[1] = cosine_of(phase + 0.75 * lon_count, lon_count)
    lon = lax.broadcasted_iota(jnp.int32, (ROWS, total), 0).astype(F32)
    phase = lon * order + offset
    factor = 1.0 / math.sqrt(lon_count)
    small[0] = cosine_of(phase, lon_count) * factor
    small[1] = cosine_of(phase + 0.75 * lon_count, lon_count) * factor


def fill(dst, big, small, count):
    def step(h, carry):
        value = big[0, pl.ds(h, 1), :] * small[0] - big[1, pl.ds(h, 1), :] * small[1]
        dst[pl.ds(pl.multiple_of(h * ROWS, ROWS), ROWS), :] = value.astype(BF16)
        return carry

    lax.fori_loop(0, count, step, 0)


def alpha_column(section, rows, span):
    row = lax.broadcasted_iota(jnp.int32, (rows, 128), 0)
    zero = jnp.logical_or(row == 0, row == span // 2)
    alpha = jnp.where(zero, 1.0, 2.0) if section == 0 else jnp.full((rows, 128), 2.0, F32)
    return alpha[:, 0:1]


def section_product(table, wide, out, section, scaled):
    _, devices, span, width = out.shape
    count = devices * span
    chunk = 256
    each = chunk // span
    for q in range(count // chunk):
        first = section * count + q * chunk
        value = jnp.dot(table[first : first + chunk, :], wide, preferred_element_type=F32)
        if scaled:
            value = value * (alpha_column(0, chunk, span) if first == 0 else 2.0)
        out[section, q * each : (q + 1) * each] = value.astype(BF16).reshape(each, span, width)


def legendre_tables(
    slot_ref, start_ref, lat_ref, synth, anal, tsynth, tanal, hold
):
    groups, width = slot_ref.shape
    orders = slot_ref[...] + lax.axis_index("space").astype(F32)
    order_sq = orders * orders
    cosine = lat_ref[0:1, :]
    wrow = lat_ref[1:2, :]
    wcol = jnp.broadcast_to(wrow, (128, width)).T[:, 0:1]
    block = 32

    def degree_block(index, carry):
        p_now, p_prev, e_prev, log_scale = carry
        scale = jnp.exp(log_scale)
        base = index * block
        for inner in range(block):
            degree_int = base + inner
            degree = degree_int.astype(F32)
            active = degree > orders
            square = degree * degree
            ratio = jnp.maximum(square - order_sq, 1.0) / jnp.maximum(4.0 * square - 1.0, 1.0)
            coef = lax.rsqrt(ratio)
            p_next = jnp.where(active, coef * (cosine * p_now - e_prev * p_prev), p_now)
            p_prev = jnp.where(active, p_now, p_prev)
            e_prev = jnp.where(active, ratio * coef, 0.0)
            p_now = p_next
            value = jnp.where(degree >= orders, p_now * scale, 0.0)
            rows = pl.ds(pl.multiple_of(degree_int * groups, groups), groups)
            for part in range(width // 128):
                hold[part, rows, :] = value[:, part * 128 : (part + 1) * 128]
        magnitude = jnp.maximum(jnp.abs(p_now), jnp.abs(p_prev))
        return (p_now / magnitude, p_prev / magnitude, e_prev, log_scale + jnp.log(magnitude))

    ones = jnp.ones((groups, width), F32)
    zeros = jnp.zeros((groups, width), F32)
    lax.fori_loop(0, MODES // block, degree_block, (ones, zeros, zeros, start_ref[...]))

    def spread(g, carry):
        pieces = [
            hold[part, pl.ds(g, MODES, stride=groups), :]
            for part in range(width // 128)
        ]
        value = pieces[0] if len(pieces) == 1 else jnp.concatenate(pieces, 1)
        synth[g] = value.astype(BF16)
        anal[g] = (value * wrow).astype(BF16)
        turned = value.T
        tsynth[g] = turned.astype(BF16)
        tanal[g] = (turned * wcol).astype(BF16)
        return carry

    lax.fori_loop(0, synth.shape[0], spread, 0)


def unpack(src, scratch, q):
    _, devices, span, _ = src.shape
    for a in range(scratch.shape[0]):
        part = src[q, :, :, a * 128 : (a + 1) * 128].astype(F32)
        scratch[a, q * devices * span : (q + 1) * devices * span] = part.reshape(devices * span, 128)


def pack(scratch, dst, q):
    _, devices, span, _ = dst.shape
    for a in range(scratch.shape[0]):
        part = scratch[a, q * devices * span : (q + 1) * devices * span]
        dst[q, :, :, a * 128 : (a + 1) * 128] = part.reshape(devices, span, 128).astype(BF16)


def strided_rows(s, r, devices, span):
    half = span // 2
    start = s // half * (devices * span) + r * half + s % half
    return pl.ds(start, devices, stride=span)


def gather_group(scratch, g, devices, span, per_group, height):
    lat_local = scratch.shape[0]
    rows = []
    for j in range(per_group):
        s = g * per_group + j
        halves = []
        for r in range(2):
            pick = strided_rows(s, r, devices, span)
            parts = [scratch[a, pick, :] for a in range(lat_local)]
            if height > devices * lat_local:
                parts.append(jnp.zeros((height - devices * lat_local, 128), F32))
            halves.append(jnp.concatenate(parts, 0))
        zero = jnp.zeros((height, 256), F32)
        cells = [zero] * per_group
        cells[j] = jnp.concatenate(halves, 1)
        rows.append(cells[0] if per_group == 1 else jnp.concatenate(cells, 1))
    return (rows[0] if per_group == 1 else jnp.concatenate(rows, 0)).astype(BF16)


def scatter_group(value, scratch, g, devices, span, per_group, height):
    lat_local = scratch.shape[0]
    for j in range(per_group):
        s = g * per_group + j
        for r in range(2):
            for a in range(lat_local):
                top = j * height + a * devices
                left = j * 256 + r * 128
                scratch[a, strided_rows(s, r, devices, span), :] = value[
                    top : top + devices, left : left + 128
                ]


def over_groups(groups, sections, section, body):
    pieces = 4
    each = groups // pieces
    share = pieces // sections
    for q in range(section * share, (section + 1) * share):
        first = q * (MODES // pieces)
        lax.fori_loop(q * each, (q + 1) * each, functools.partial(body, first), 0)


def widen(filter_ref, first, copies):
    gain = filter_ref[first:, :].astype(F32)
    return jnp.concatenate([gain] * copies, 1)


def forward_body(per_group, shapes, anal, tsynth, filt, weight, scratch, back):
    _, devices, span, _ = shapes
    height = anal.shape[2] // per_group

    def body(first, g, carry):
        operand = gather_group(scratch, g, devices, span, per_group, height)
        spectrum = jnp.dot(anal[g, first:, :], operand, preferred_element_type=F32).astype(BF16)
        scaled = (spectrum.astype(F32) * widen(filt, first, 2 * per_group)).astype(BF16)
        mixed = [
            jnp.dot(
                scaled[:, j * 256 : (j + 1) * 256], weight[...], preferred_element_type=F32
            ).astype(BF16)
            for j in range(per_group)
        ]
        mixed = mixed[0] if per_group == 1 else jnp.concatenate(mixed, 1)
        value = jnp.dot(tsynth[g, :, first:], mixed, preferred_element_type=F32)
        scatter_group(value, back, g, devices, span, per_group, height)
        return carry

    return body


def backward_body(
    per_group, shapes, anal, synth, tanal, filt, weight, scratch, gscratch, wgrad, fgrad
):
    _, devices, span, _ = shapes
    height = anal.shape[2] // per_group

    def body(first, g, carry):
        operand = gather_group(scratch, g, devices, span, per_group, height)
        goperand = gather_group(gscratch, g, devices, span, per_group, height)
        gain = widen(filt, first, 2)
        outs = []
        spectrum = jnp.dot(anal[g, first:, :], operand, preferred_element_type=F32).astype(BF16)
        gmixed = jnp.dot(synth[g, first:, :], goperand, preferred_element_type=F32).astype(BF16)
        for j in range(per_group):
            lanes = slice(j * 256, (j + 1) * 256)
            spec = spectrum[:, lanes].astype(F32)
            scaled = (spec * gain).astype(BF16)
            gmix = gmixed[:, lanes]
            wgrad[...] += lax.dot_general(
                scaled, gmix, (((0,), (0,)), ((), ())), preferred_element_type=F32
            )
            gscaled = lax.dot_general(
                gmix, weight[...], (((1,), (1,)), ((), ())), preferred_element_type=F32
            )
            term = gscaled * spec
            fgrad[first:, :] += term[:, :128] + term[:, 128:]
            outs.append((gscaled * gain).astype(BF16))
        gspectrum = outs[0] if per_group == 1 else jnp.concatenate(outs, 1)
        value = jnp.dot(tanal[g, :, first:], gspectrum, preferred_element_type=F32)
        scatter_group(value, scratch, g, devices, span, per_group, height)
        return carry

    return body


def fold_gradients(wgrad, fgrad, red):
    half = wgrad.shape[0] // 2
    pieces = [
        (wgrad[:half, :half] + wgrad[half:, half:]) * (1.0 / MODES),
        (wgrad[:half, half:] - wgrad[half:, :half]) * (1.0 / MODES),
        fgrad[...] * 0.125,
    ]
    spare = red.shape[0] * red.shape[1] - 2 * half - MODES
    if spare:
        pieces.append(jnp.zeros((spare, 128), F32))
    red[...] = jnp.concatenate(pieces, 0).reshape(red.shape)


def gelu_slope(field):
    return 0.5 * (1.0 + lax.erf(field * (1.0 / math.sqrt(2.0)))) + field * jnp.exp(
        -0.5 * field * field
    ) * (1.0 / math.sqrt(2.0 * math.pi))


LON_CHUNK = 288


def merged(src, section):
    _, devices, span, width = src.shape
    return src[section].astype(F32).reshape(devices * span, width)


def add_section(ttable, operand, section, field, last):
    count = operand.shape[0]
    lon_count = field.shape[0]

    def grid_rows(q, carry):
        rows = pl.ds(pl.multiple_of(q * LON_CHUNK, LON_CHUNK), LON_CHUNK)
        value = jnp.dot(
            ttable[rows, section * count : (section + 1) * count],
            operand,
            preferred_element_type=F32,
        )
        if section:
            value = value + field[rows, :]
        if last is None:
            field[rows, :] = value
        else:
            last(rows, value)
        return carry

    lax.fori_loop(0, lon_count // LON_CHUNK, grid_rows, 0)


def block_kernel(
    per_group,
    columns, lanes, grid, upstream, slots, start, lats, filt, mix_weight,
    grad, grad_weight, grad_filter,
    weight, total, table, ttable, big, small, tbig, tsmall,
    synth, anal, tsynth, tanal, hold,
    out1, in1, out2, in2, out3, in3, out4, in4,
    scratch, back, field, slope, wgrad, fgrad, red, inbox,
    send1, recv1, send2, recv2, send3, recv3, send4, recv4, rsend, rrecv,
):
    shapes = out1.shape
    sections, devices, span, _ = shapes
    lat_local, lon_count, channels = grid.shape
    groups = synth.shape[0]
    greet(devices)
    weight[:channels, :channels] = mix_weight[0]
    weight[:channels, channels:] = mix_weight[1]
    weight[channels:, :channels] = -mix_weight[1]
    weight[channels:, channels:] = mix_weight[0]
    angles_by_row(columns, lon_count, big, small)
    fill(table, big, small, big.shape[1])

    first = Exchange(out1, in1, send1, recv1)
    wide = jnp.concatenate([grid[a] for a in range(lat_local)], 1)
    for q in range(sections):
        section_product(table, wide, out1, q, False)
        if q == 0:
            await_greetings(devices)
        first.send(q)
    legendre_tables(slots, start, lats, synth, anal, tsynth, tanal, hold)
    angles_by_lane(lanes, lon_count, tbig, tsmall)
    fill(ttable, tbig, tsmall, tbig.shape[1])

    second = Exchange(out2, in2, send2, recv2)
    forward = forward_body(per_group, shapes, anal, tsynth, filt, weight, scratch, back)
    for q in range(sections):
        first.arrive(q)
        unpack(in1, scratch, q)
        over_groups(groups, sections, q, forward)
        pack(back, out2, q)
        second.send(q)

    def gate(rows, value):
        up = jnp.concatenate([upstream[a, rows, :] for a in range(lat_local)], 1)
        slope[rows, :] = (up.astype(F32) * gelu_slope(value)).astype(BF16)

    for q in range(sections):
        second.arrive(q)
        operand = merged(in2, q)
        operand = (operand * alpha_column(q, operand.shape[0], span)).astype(BF16)
        add_section(ttable, operand, q, field, gate if q == sections - 1 else None)

    third = Exchange(out3, in3, send3, recv3)
    for q in range(sections):
        section_product(table, slope[...], out3, q, True)
        third.send(q)

    wgrad[...] = jnp.zeros_like(wgrad)
    fgrad[...] = jnp.zeros_like(fgrad)
    fourth = Exchange(out4, in4, send4, recv4)
    backward = backward_body(
        per_group, shapes, anal, synth, tanal, filt, weight, scratch, back, wgrad, fgrad
    )
    for q in range(sections):
        third.arrive(q)
        unpack(in3, back, q)
        over_groups(groups, sections, q, backward)
        pack(scratch, out4, q)
        if q == 0:
            fourth.send(q)
    fold_gradients(wgrad, fgrad, red)
    reduction = Reduction(red, inbox, total, rsend, rrecv)
    reduction.scatter([functools.partial(fourth.send, q) for q in range(1, sections)])

    def finish(rows, value):
        for a in range(lat_local):
            part = value[:, a * channels : (a + 1) * channels]
            grad[a, rows, :] = (part + upstream[a, rows, :].astype(F32)).astype(BF16)

    hops = len(reduction.hops)
    for step in range(max(hops, sections)):
        copy = reduction.gather(step) if step < hops else None
        if step < sections:
            fourth.arrive(step)
            add_section(
                ttable,
                merged(in4, step).astype(BF16),
                step,
                field,
                finish if step == sections - 1 else None,
            )
        if copy is not None:
            copy.wait()
    sums = total[...].reshape(-1, channels)
    for r in range(2):
        grad_weight[r] = sums[r * channels : (r + 1) * channels]
    grad_filter[...] = sums[2 * channels : 2 * channels + MODES]
    for exchange in (first, second, third, fourth):
        exchange.drain()


def body(grid_in, upstream, mix_weight, degree_filter):
    devices = lax.axis_size("space")
    me = lax.axis_index("space")
    lat_local, lon_count, channels = grid_in.shape
    lat_count = lat_local * devices
    slots = MODES // devices
    sections = sections_of(devices)
    span = 2 * slots // sections
    height = 64 if lat_count <= 64 else -(-lat_count // 128) * 128
    per_group = 128 // height if height < 128 else 1
    width = height * per_group
    groups = slots // per_group
    dims = (sections, devices, span, lat_local * channels)

    lane = np.arange(width)
    within = lane % height
    valid = within < lat_count
    latitude = np.where(valid, within % devices * lat_local + within // devices, 0)
    padded = -(-groups // 8) * 8
    group = np.minimum(np.arange(padded), groups - 1)[:, None]
    slot_orders = ((group * per_group + lane[None, :] // height) * devices).astype(np.float32)
    slot_orders = jnp.asarray(slot_orders)
    angles = latitude_angles(jnp.asarray(latitude), lat_count)
    orders = slot_orders + me.astype(F32)
    start = 0.5 * (jnp.log(2.0 * orders + 1.0) - math.log(2.0))
    start = start + 0.5 * (
        lax.lgamma(2.0 * orders + 1.0) - 2.0 * lax.lgamma(orders + 1.0) - orders * math.log(4.0)
    )
    start = start + orders * jnp.log(jnp.sin(angles))[None, :]
    row = jnp.arange(8)[:, None]
    weights = math.pi / lat_count * jnp.sin(angles) * jnp.asarray(valid.astype(np.float32))
    lats = jnp.where(row == 0, jnp.cos(angles)[None, :], weights[None, :])

    share = -(-(2 * channels + MODES) // (8 * devices)) * 8
    blocks = (devices, share, channels)
    vmem = pltpu.VMEM
    slab = vmem((lat_local, 2 * MODES, 128), F32)
    total_rows = 2 * MODES
    semaphores = pltpu.SemaphoreType.DMA((sections, devices))
    hops = pltpu.SemaphoreType.DMA((2 * devices.bit_length(),))
    return pl.pallas_call(
        functools.partial(block_kernel, per_group),
        out_shape=(
            jax.ShapeDtypeStruct(grid_in.shape, BF16),
            jax.ShapeDtypeStruct(mix_weight.shape, F32),
            jax.ShapeDtypeStruct(degree_filter.shape, F32),
        ),
        scratch_shapes=[
            vmem((2 * channels, 2 * channels), BF16),
            vmem(blocks, F32),
            vmem((total_rows, lon_count), BF16),
            vmem((lon_count, total_rows), BF16),
            vmem((2, total_rows // ROWS, lon_count), F32),
            vmem((2, ROWS, lon_count), F32),
            vmem((2, lon_count // ROWS, total_rows), F32),
            vmem((2, ROWS, total_rows), F32),
            vmem((groups, MODES, width), BF16),
            vmem((groups, MODES, width), BF16),
            vmem((groups, width, MODES), BF16),
            vmem((groups, width, MODES), BF16),
            vmem((width // 128, MODES * padded, 128), F32),
            *[vmem(dims, BF16)] * 8,
            slab,
            slab,
            vmem((lon_count, lat_local * channels), F32),
            vmem((lon_count, lat_local * channels), BF16),
            vmem((2 * channels, 2 * channels), F32),
            vmem((MODES, channels), F32),
            vmem(blocks, F32),
            vmem(blocks, F32),
            *[semaphores] * 8,
            hops,
            hops,
        ],
        compiler_params=params(collective_id=0, has_side_effects=True),
        name="block",
    )(
        *angle_indices(devices, lon_count),
        grid_in,
        upstream,
        slot_orders,
        start,
        lats,
        degree_filter,
        mix_weight,
    )


def solution(mesh):
    return jax.shard_map(
        body,
        mesh=mesh,
        in_specs=(P(("groups", "space"), None, None), P(("groups", "space"), None, None), P(), P()),
        out_specs=(P(("groups", "space"), None, None), P("groups", None, None), P("groups", None)),
        check_vma=False,
    )
```

```python
import functools
import math

import jax
import jax.numpy as jnp
import numpy as np
from jax import lax
from jax.experimental import pallas as pl
from jax.experimental.pallas import tpu as pltpu
from jax.sharding import PartitionSpec as P

MODES = 512
ROWS = 32
F32 = jnp.float32
BF16 = jnp.bfloat16


def params(**extra):
    return pltpu.CompilerParams(vmem_limit_bytes=56 * 1024 * 1024, **extra)


def latitude_angles(index, lat_count):
    return math.pi * (index.astype(F32) + 0.5) / lat_count


def greet(devices):
    me = lax.axis_index("space")
    barrier = pltpu.get_barrier_semaphore()

    def hello(step, carry):
        peer = (me + step) % devices
        pl.semaphore_signal(
            barrier, inc=1, device_id={"space": peer}, device_id_type=pl.DeviceIdType.MESH
        )
        return carry

    lax.fori_loop(1, devices, hello, 0)


def await_greetings(devices):
    pl.semaphore_wait(pltpu.get_barrier_semaphore(), devices - 1)


def remote(src, dst, send_sem, recv_sem, peer):
    return pltpu.make_async_remote_copy(
        src_ref=src,
        dst_ref=dst,
        send_sem=send_sem,
        recv_sem=recv_sem,
        device_id={"space": peer},
        device_id_type=pl.DeviceIdType.MESH,
    )


class Exchange:
    def __init__(self, source, target, send_sem, recv_sem):
        self.source, self.target = source, target
        self.send_sem, self.recv_sem = send_sem, recv_sem
        self.devices = source.shape[1]
        self.me = lax.axis_index("space")

    def copy(self, section, step):
        peer = (self.me + step) % self.devices
        return remote(
            self.source.at[section, peer],
            self.target.at[section, self.me],
            self.send_sem.at[section, step],
            self.recv_sem.at[section, step],
            peer,
        )

    def send(self, section):
        half = self.devices // 2

        def one(index, carry):
            sign = 1 - 2 * (index % 2)
            step = (half + sign * ((index + 1) // 2) + self.devices) % self.devices
            self.copy(section, step).start()
            return carry

        lax.fori_loop(0, self.devices - 1, one, 0)
        self.target[section, self.me] = self.source[section, self.me]

    def arrive(self, section):
        def one(step, carry):
            self.copy(section, step).wait_recv()
            return carry

        lax.fori_loop(1, self.devices, one, 0)

    def drain(self):
        for section in range(self.source.shape[0]):

            def one(step, carry, section=section):
                self.copy(section, step).wait_send()
                return carry

            lax.fori_loop(1, self.devices, one, 0)


class Reduction:
    def __init__(self, red, inbox, total, send_sem, recv_sem):
        self.red, self.inbox, self.total = red, inbox, total
        self.send_sem, self.recv_sem = send_sem, recv_sem
        devices = red.shape[0]
        me = lax.axis_index("space")
        self.hops = []
        base = me * 0
        stride = 1
        while stride < devices:
            half = devices // (2 * stride)
            bit = me // stride % 2
            keep, give = base + bit * half, base + (1 - bit) * half
            self.hops.append((half, keep, give, me + (1 - 2 * bit) * stride))
            base = keep
            stride *= 2
        self.base = base

    def scatter(self, held):
        count = len(self.hops)
        early = max(1, len(held) - 2) if held else 0
        for send in held[:early]:
            send()
        late = held[early:]
        for t, (half, keep, give, partner) in enumerate(self.hops):
            copy = remote(
                self.red.at[pl.ds(give, half)],
                self.inbox.at[pl.ds(half, half)],
                self.send_sem.at[t],
                self.recv_sem.at[t],
                partner,
            )
            copy.start()
            index = t - (count - len(late))
            if index >= 0:
                late[index]()
            copy.wait()
            self.red[pl.ds(keep, half)] += self.inbox[half : 2 * half]
        self.total[pl.ds(self.base, 1)] = self.red[pl.ds(self.base, 1)]

    def gather(self, index):
        count = len(self.hops)
        t = count - 1 - index
        half, keep, _, partner = self.hops[t]
        block = self.total.at[pl.ds(keep, half)]
        copy = remote(
            block, block, self.send_sem.at[count + t], self.recv_sem.at[count + t], partner
        )
        copy.start()
        return copy


def sections_of(devices):
    return max(1, min(4, MODES // devices // 8))


def row_phase(rows, devices, lon_count):
    span = 2 * MODES // devices // sections_of(devices)
    section = rows // (span * devices)
    device = rows // span % devices
    part = rows // (span // 2) % 2
    slot = section * (span // 2) + rows % (span // 2)
    return slot * devices + device, part * (lon_count // 4)


def cosine_of(phase, lon_count):
    turn = phase - jnp.floor(phase * (1.0 / lon_count)) * lon_count
    x = (lon_count / 4 - jnp.abs(turn - lon_count / 2)) * (2.0 * math.pi / lon_count)
    y = x * x
    tail = 1.0 / 362880.0 - y * (1.0 / 39916800.0)
    tail = 1.0 / 120.0 + y * (-1.0 / 5040.0 + y * tail)
    return -x * (1.0 + y * (-1.0 / 6.0 + y * tail))


def angle_indices(devices, lon_count):
    order, offset = row_phase(np.arange(2 * MODES), devices, lon_count)

    def column(values):
        return np.broadcast_to(values.astype(np.float32)[:, None], (len(values), 128))

    def lanes(values):
        return np.broadcast_to(values.astype(np.float32)[None, :], (8, len(values)))

    columns = np.stack([column(v) for v in (order[::ROWS], offset[::ROWS], order[:ROWS], offset[:ROWS])])
    return jnp.asarray(columns), jnp.asarray(np.stack([lanes(order), lanes(offset)]))


def angles_by_row(columns, lon_count, big, small):
    rows = big.shape[1]
    lon = lax.broadcasted_iota(jnp.int32, (rows, lon_count), 1).astype(F32)
    phase = columns[0][:, 0:1] * lon + columns[1][:, 0:1]
    big[0] = cosine_of(phase, lon_count)
    big[1] = cosine_of(phase + 0.75 * lon_count, lon_count)
    lon = lax.broadcasted_iota(jnp.int32, (ROWS, lon_count), 1).astype(F32)
    phase = columns[2][:, 0:1] * lon + columns[3][:, 0:1]
    factor = 1.0 / math.sqrt(lon_count)
    small[0] = cosine_of(phase, lon_count) * factor
    small[1] = cosine_of(phase + 0.75 * lon_count, lon_count) * factor


def angles_by_lane(lanes, lon_count, big, small):
    rows, total = big.shape[1:]
    order, offset = lanes[0, 0:1, :], lanes[1, 0:1, :]
    lon = lax.broadcasted_iota(jnp.int32, (rows, total), 0).astype(F32) * float(ROWS)
    phase = lon * order
    big[0] = cosine_of(phase, lon_count)
    big[1] = cosine_of(phase + 0.75 * lon_count, lon_count)
    lon = lax.broadcasted_iota(jnp.int32, (ROWS, total), 0).astype(F32)
    phase = lon * order + offset
    factor = 1.0 / math.sqrt(lon_count)
    small[0] = cosine_of(phase, lon_count) * factor
    small[1] = cosine_of(phase + 0.75 * lon_count, lon_count) * factor


def fill(dst, big, small, count):
    def step(h, carry):
        value = big[0, pl.ds(h, 1), :] * small[0] - big[1, pl.ds(h, 1), :] * small[1]
        dst[pl.ds(pl.multiple_of(h * ROWS, ROWS), ROWS), :] = value.astype(BF16)
        return carry

    lax.fori_loop(0, count, step, 0)


def alpha_column(section, rows, span):
    row = lax.broadcasted_iota(jnp.int32, (rows, 128), 0)
    zero = jnp.logical_or(row == 0, row == span // 2)
    alpha = jnp.where(zero, 1.0, 2.0) if section == 0 else jnp.full((rows, 128), 2.0, F32)
    return alpha[:, 0:1]


def section_product(table, wide, out, section, scaled):
    _, devices, span, width = out.shape
    count = devices * span
    chunk = 256
    each = chunk // span
    for q in range(count // chunk):
        first = section * count + q * chunk
        value = jnp.dot(table[first : first + chunk, :], wide, preferred_element_type=F32)
        if scaled:
            value = value * (alpha_column(0, chunk, span) if first == 0 else 2.0)
        out[section, q * each : (q + 1) * each] = value.astype(BF16).reshape(each, span, width)


def legendre_tables(
    slot_ref, start_ref, lat_ref, synth, anal, tsynth, tanal, hold
):
    groups, width = slot_ref.shape
    orders = slot_ref[...] + lax.axis_index("space").astype(F32)
    order_sq = orders * orders
    cosine = lat_ref[0:1, :]
    wrow = lat_ref[1:2, :]
    wcol = jnp.broadcast_to(wrow, (128, width)).T[:, 0:1]
    block = 32

    def degree_block(index, carry):
        p_now, p_prev, e_prev, log_scale = carry
        scale = jnp.exp(log_scale)
        base = index * block
        for inner in range(block):
            degree_int = base + inner
            degree = degree_int.astype(F32)
            active = degree > orders
            square = degree * degree
            ratio = jnp.maximum(square - order_sq, 1.0) / jnp.maximum(4.0 * square - 1.0, 1.0)
            coef = lax.rsqrt(ratio)
            p_next = jnp.where(active, coef * (cosine * p_now - e_prev * p_prev), p_now)
            p_prev = jnp.where(active, p_now, p_prev)
            e_prev = jnp.where(active, ratio * coef, 0.0)
            p_now = p_next
            value = jnp.where(degree >= orders, p_now * scale, 0.0)
            rows = pl.ds(pl.multiple_of(degree_int * groups, groups), groups)
            for part in range(width // 128):
                hold[part, rows, :] = value[:, part * 128 : (part + 1) * 128]
        magnitude = jnp.maximum(jnp.abs(p_now), jnp.abs(p_prev))
        return (p_now / magnitude, p_prev / magnitude, e_prev, log_scale + jnp.log(magnitude))

    ones = jnp.ones((groups, width), F32)
    zeros = jnp.zeros((groups, width), F32)
    lax.fori_loop(0, MODES // block, degree_block, (ones, zeros, zeros, start_ref[...]))

    def spread(g, carry):
        pieces = [
            hold[part, pl.ds(g, MODES, stride=groups), :]
            for part in range(width // 128)
        ]
        value = pieces[0] if len(pieces) == 1 else jnp.concatenate(pieces, 1)
        synth[g] = value.astype(BF16)
        anal[g] = (value * wrow).astype(BF16)
        turned = value.T
        tsynth[g] = turned.astype(BF16)
        tanal[g] = (turned * wcol).astype(BF16)
        return carry

    lax.fori_loop(0, synth.shape[0], spread, 0)


def unpack(src, scratch, q):
    _, devices, span, _ = src.shape
    for a in range(scratch.shape[0]):
        part = src[q, :, :, a * 128 : (a + 1) * 128].astype(F32)
        scratch[a, q * devices * span : (q + 1) * devices * span] = part.reshape(devices * span, 128)


def pack(scratch, dst, q):
    _, devices, span, _ = dst.shape
    for a in range(scratch.shape[0]):
        part = scratch[a, q * devices * span : (q + 1) * devices * span]
        dst[q, :, :, a * 128 : (a + 1) * 128] = part.reshape(devices, span, 128).astype(BF16)


def strided_rows(s, r, devices, span):
    half = span // 2
    start = s // half * (devices * span) + r * half + s % half
    return pl.ds(start, devices, stride=span)


def gather_group(scratch, g, devices, span, per_group, height):
    lat_local = scratch.shape[0]
    rows = []
    for j in range(per_group):
        s = g * per_group + j
        halves = []
        for r in range(2):
            pick = strided_rows(s, r, devices, span)
            parts = [scratch[a, pick, :] for a in range(lat_local)]
            if height > devices * lat_local:
                parts.append(jnp.zeros((height - devices * lat_local, 128), F32))
            halves.append(jnp.concatenate(parts, 0))
        zero = jnp.zeros((height, 256), F32)
        cells = [zero] * per_group
        cells[j] = jnp.concatenate(halves, 1)
        rows.append(cells[0] if per_group == 1 else jnp.concatenate(cells, 1))
    return (rows[0] if per_group == 1 else jnp.concatenate(rows, 0)).astype(BF16)


def scatter_group(value, scratch, g, devices, span, per_group, height):
    lat_local = scratch.shape[0]
    for j in range(per_group):
        s = g * per_group + j
        for r in range(2):
            for a in range(lat_local):
                top = j * height + a * devices
                left = j * 256 + r * 128
                scratch[a, strided_rows(s, r, devices, span), :] = value[
                    top : top + devices, left : left + 128
                ]


def over_groups(groups, sections, section, body):
    pieces = 4
    each = groups // pieces
    share = pieces // sections
    for q in range(section * share, (section + 1) * share):
        first = q * (MODES // pieces)
        pair = 2 if each % 2 == 0 else 1

        def step(index, carry, first=first, pair=pair, q=q):
            for j in range(pair):
                body(first, q * each + index * pair + j, carry)
            return carry

        lax.fori_loop(0, each // pair, step, 0)


def widen(filter_ref, first, copies):
    gain = filter_ref[first:, :].astype(F32)
    return jnp.concatenate([gain] * copies, 1)


def forward_body(per_group, shapes, anal, tsynth, filt, weight, scratch, back):
    _, devices, span, _ = shapes
    height = anal.shape[2] // per_group

    def body(first, g, carry):
        operand = gather_group(scratch, g, devices, span, per_group, height)
        spectrum = jnp.dot(anal[g, first:, :], operand, preferred_element_type=F32).astype(BF16)
        scaled = (spectrum.astype(F32) * widen(filt, first, 2 * per_group)).astype(BF16)
        mixed = [
            jnp.dot(
                scaled[:, j * 256 : (j + 1) * 256], weight[...], preferred_element_type=F32
            ).astype(BF16)
            for j in range(per_group)
        ]
        mixed = mixed[0] if per_group == 1 else jnp.concatenate(mixed, 1)
        value = jnp.dot(tsynth[g, :, first:], mixed, preferred_element_type=F32)
        scatter_group(value, back, g, devices, span, per_group, height)
        return carry

    return body


def backward_body(
    per_group, shapes, anal, synth, tanal, filt, weight, scratch, gscratch, wgrad, fgrad
):
    _, devices, span, _ = shapes
    height = anal.shape[2] // per_group

    def body(first, g, carry):
        operand = gather_group(scratch, g, devices, span, per_group, height)
        goperand = gather_group(gscratch, g, devices, span, per_group, height)
        gain = widen(filt, first, 2)
        outs = []
        spectrum = jnp.dot(anal[g, first:, :], operand, preferred_element_type=F32).astype(BF16)
        gmixed = jnp.dot(synth[g, first:, :], goperand, preferred_element_type=F32).astype(BF16)
        for j in range(per_group):
            lanes = slice(j * 256, (j + 1) * 256)
            spec = spectrum[:, lanes].astype(F32)
            scaled = (spec * gain).astype(BF16)
            gmix = gmixed[:, lanes]
            wgrad[...] += lax.dot_general(
                scaled, gmix, (((0,), (0,)), ((), ())), preferred_element_type=F32
            )
            gscaled = lax.dot_general(
                gmix, weight[...], (((1,), (1,)), ((), ())), preferred_element_type=F32
            )
            term = gscaled * spec
            fgrad[first:, :] += term[:, :128] + term[:, 128:]
            outs.append((gscaled * gain).astype(BF16))
        gspectrum = outs[0] if per_group == 1 else jnp.concatenate(outs, 1)
        value = jnp.dot(tanal[g, :, first:], gspectrum, preferred_element_type=F32)
        scatter_group(value, scratch, g, devices, span, per_group, height)
        return carry

    return body


def fold_gradients(wgrad, fgrad, red):
    half = wgrad.shape[0] // 2
    pieces = [
        (wgrad[:half, :half] + wgrad[half:, half:]) * (1.0 / MODES),
        (wgrad[:half, half:] - wgrad[half:, :half]) * (1.0 / MODES),
        fgrad[...] * 0.125,
    ]
    spare = red.shape[0] * red.shape[1] - 2 * half - MODES
    if spare:
        pieces.append(jnp.zeros((spare, 128), F32))
    red[...] = jnp.concatenate(pieces, 0).reshape(red.shape)


def gelu_slope(field):
    return 0.5 * (1.0 + lax.erf(field * (1.0 / math.sqrt(2.0)))) + field * jnp.exp(
        -0.5 * field * field
    ) * (1.0 / math.sqrt(2.0 * math.pi))


LON_CHUNK = 288


def merged(src, section):
    _, devices, span, width = src.shape
    return src[section].astype(F32).reshape(devices * span, width)


def add_section(ttable, operand, section, field, last):
    count = operand.shape[0]
    lon_count = field.shape[0]

    def grid_rows(q, carry):
        rows = pl.ds(pl.multiple_of(q * LON_CHUNK, LON_CHUNK), LON_CHUNK)
        value = jnp.dot(
            ttable[rows, section * count : (section + 1) * count],
            operand,
            preferred_element_type=F32,
        )
        if section:
            value = value + field[rows, :]
        if last is None:
            field[rows, :] = value
        else:
            last(rows, value)
        return carry

    lax.fori_loop(0, lon_count // LON_CHUNK, grid_rows, 0)


def block_kernel(
    per_group,
    columns, lanes, grid, upstream, slots, start, lats, filt, mix_weight,
    grad, grad_weight, grad_filter,
    weight, total, table, ttable, big, small, tbig, tsmall,
    synth, anal, tsynth, tanal, hold,
    out1, in1, out2, in2, out3, in3, out4, in4,
    scratch, back, field, slope, wgrad, fgrad, red, inbox,
    send1, recv1, send2, recv2, send3, recv3, send4, recv4, rsend, rrecv,
):
    shapes = out1.shape
    sections, devices, span, _ = shapes
    lat_local, lon_count, channels = grid.shape
    groups = synth.shape[0]
    greet(devices)
    weight[:channels, :channels] = mix_weight[0]
    weight[:channels, channels:] = mix_weight[1]
    weight[channels:, :channels] = -mix_weight[1]
    weight[channels:, channels:] = mix_weight[0]
    angles_by_row(columns, lon_count, big, small)
    fill(table, big, small, big.shape[1])

    first = Exchange(out1, in1, send1, recv1)
    wide = jnp.concatenate([grid[a] for a in range(lat_local)], 1)
    for q in range(sections):
        section_product(table, wide, out1, q, False)
        if q == 0:
            await_greetings(devices)
        first.send(q)
    legendre_tables(slots, start, lats, synth, anal, tsynth, tanal, hold)
    angles_by_lane(lanes, lon_count, tbig, tsmall)
    fill(ttable, tbig, tsmall, tbig.shape[1])

    second = Exchange(out2, in2, send2, recv2)
    forward = forward_body(per_group, shapes, anal, tsynth, filt, weight, scratch, back)
    for q in range(sections):
        first.arrive(q)
        unpack(in1, scratch, q)
        over_groups(groups, sections, q, forward)
        pack(back, out2, q)
        second.send(q)

    def gate(rows, value):
        up = jnp.concatenate([upstream[a, rows, :] for a in range(lat_local)], 1)
        slope[rows, :] = (up.astype(F32) * gelu_slope(value)).astype(BF16)

    for q in range(sections):
        second.arrive(q)
        operand = merged(in2, q)
        operand = (operand * alpha_column(q, operand.shape[0], span)).astype(BF16)
        add_section(ttable, operand, q, field, gate if q == sections - 1 else None)

    third = Exchange(out3, in3, send3, recv3)
    for q in range(sections):
        section_product(table, slope[...], out3, q, True)
        third.send(q)

    wgrad[...] = jnp.zeros_like(wgrad)
    fgrad[...] = jnp.zeros_like(fgrad)
    fourth = Exchange(out4, in4, send4, recv4)
    backward = backward_body(
        per_group, shapes, anal, synth, tanal, filt, weight, scratch, back, wgrad, fgrad
    )
    for q in range(sections):
        third.arrive(q)
        unpack(in3, back, q)
        over_groups(groups, sections, q, backward)
        pack(scratch, out4, q)
        if q == 0:
            fourth.send(q)
    fold_gradients(wgrad, fgrad, red)
    reduction = Reduction(red, inbox, total, rsend, rrecv)
    reduction.scatter([functools.partial(fourth.send, q) for q in range(1, sections)])

    def finish(rows, value):
        for a in range(lat_local):
            part = value[:, a * channels : (a + 1) * channels]
            grad[a, rows, :] = (part + upstream[a, rows, :].astype(F32)).astype(BF16)

    hops = len(reduction.hops)
    for step in range(max(hops, sections)):
        copy = reduction.gather(step) if step < hops else None
        if step < sections:
            fourth.arrive(step)
            add_section(
                ttable,
                merged(in4, step).astype(BF16),
                step,
                field,
                finish if step == sections - 1 else None,
            )
        if copy is not None:
            copy.wait()
    sums = total[...].reshape(-1, channels)
    for r in range(2):
        grad_weight[r] = sums[r * channels : (r + 1) * channels]
    grad_filter[...] = sums[2 * channels : 2 * channels + MODES]
    for exchange in (first, second, third, fourth):
        exchange.drain()


def body(grid_in, upstream, mix_weight, degree_filter):
    devices = lax.axis_size("space")
    me = lax.axis_index("space")
    lat_local, lon_count, channels = grid_in.shape
    lat_count = lat_local * devices
    slots = MODES // devices
    sections = sections_of(devices)
    span = 2 * slots // sections
    height = 64 if lat_count <= 64 else -(-lat_count // 128) * 128
    per_group = 128 // height if height < 128 else 1
    width = height * per_group
    groups = slots // per_group
    dims = (sections, devices, span, lat_local * channels)

    lane = np.arange(width)
    within = lane % height
    valid = within < lat_count
    latitude = np.where(valid, within % devices * lat_local + within // devices, 0)
    padded = -(-groups // 8) * 8
    group = np.minimum(np.arange(padded), groups - 1)[:, None]
    slot_orders = ((group * per_group + lane[None, :] // height) * devices).astype(np.float32)
    slot_orders = jnp.asarray(slot_orders)
    angles = latitude_angles(jnp.asarray(latitude), lat_count)
    orders = slot_orders + me.astype(F32)
    start = 0.5 * (jnp.log(2.0 * orders + 1.0) - math.log(2.0))
    start = start + 0.5 * (
        lax.lgamma(2.0 * orders + 1.0) - 2.0 * lax.lgamma(orders + 1.0) - orders * math.log(4.0)
    )
    start = start + orders * jnp.log(jnp.sin(angles))[None, :]
    row = jnp.arange(8)[:, None]
    weights = math.pi / lat_count * jnp.sin(angles) * jnp.asarray(valid.astype(np.float32))
    lats = jnp.where(row == 0, jnp.cos(angles)[None, :], weights[None, :])

    share = -(-(2 * channels + MODES) // (8 * devices)) * 8
    blocks = (devices, share, channels)
    vmem = pltpu.VMEM
    slab = vmem((lat_local, 2 * MODES, 128), F32)
    total_rows = 2 * MODES
    semaphores = pltpu.SemaphoreType.DMA((sections, devices))
    hops = pltpu.SemaphoreType.DMA((2 * devices.bit_length(),))
    return pl.pallas_call(
        functools.partial(block_kernel, per_group),
        out_shape=(
            jax.ShapeDtypeStruct(grid_in.shape, BF16),
            jax.ShapeDtypeStruct(mix_weight.shape, F32),
            jax.ShapeDtypeStruct(degree_filter.shape, F32),
        ),
        scratch_shapes=[
            vmem((2 * channels, 2 * channels), BF16),
            vmem(blocks, F32),
            vmem((total_rows, lon_count), BF16),
            vmem((lon_count, total_rows), BF16),
            vmem((2, total_rows // ROWS, lon_count), F32),
            vmem((2, ROWS, lon_count), F32),
            vmem((2, lon_count // ROWS, total_rows), F32),
            vmem((2, ROWS, total_rows), F32),
            vmem((groups, MODES, width), BF16),
            vmem((groups, MODES, width), BF16),
            vmem((groups, width, MODES), BF16),
            vmem((groups, width, MODES), BF16),
            vmem((width // 128, MODES * padded, 128), F32),
            *[vmem(dims, BF16)] * 8,
            slab,
            slab,
            vmem((lon_count, lat_local * channels), F32),
            vmem((lon_count, lat_local * channels), BF16),
            vmem((2 * channels, 2 * channels), F32),
            vmem((MODES, channels), F32),
            vmem(blocks, F32),
            vmem(blocks, F32),
            *[semaphores] * 8,
            hops,
            hops,
        ],
        compiler_params=params(collective_id=0, has_side_effects=True),
        name="block",
    )(
        *angle_indices(devices, lon_count),
        grid_in,
        upstream,
        slot_orders,
        start,
        lats,
        degree_filter,
        mix_weight,
    )


def solution(mesh):
    return jax.shard_map(
        body,
        mesh=mesh,
        in_specs=(P(("groups", "space"), None, None), P(("groups", "space"), None, None), P(), P()),
        out_specs=(P(("groups", "space"), None, None), P("groups", None, None), P("groups", None)),
        check_vma=False,
    )
```
